128 devices in a mesh: vol: 32 (over y, x, core), surf: 4 (over z).
Axes of the slice: x: 4, y: 4, z: 4, core: 2. Of those that a mesh axis runs over, the one named last changes fastest.
Arguments:
- node_pos: float32 [2048, 3, 128], P('vol'), may hold values from -6 to 6
- centres: float32 [8192, 3, 128], P(('vol', 'surf')), may hold values from -6 to 6
- coefs: float32 [8192, 3, 128], P(('vol', 'surf')), may hold values from -0.3 to 0.3
- radii: float32 [8192, 128], P(('vol', 'surf')), may hold values from 3 to 6
- block_list: int32 [4, 2048, 16], P('surf', 'vol'), may hold values from 0 to 8191, as said below
- neighbours: int32 [2048, 8], P('vol'), may hold values from 0 to 2047, as said below
- faces: int32 [2048, 3, 256], P('vol'), may hold values from 0 to 1023
Outputs:
- velocity: float32 [2048, 3, 128], P('vol')
- swept: float32 [2048, 256], P('vol')
The draws below stay inside these ranges and needn't reach their ends.
Inputs may be any that keep to these rules, and one draw needn't show every extreme that they name: `block_list`: A value g names block g % 64 of device g // 64 in the flat order of vol+surf. The 1024 entries held by one device name blocks of every device exactly 8 times; the 16 entries of one box on one device name blocks of distinct devices. `neighbours`: every entry of box b names a box within 4 of b.
All inputs are finite; a program needn't handle non-finite values.
Results may differ from the reference program's by a relative error of at most 0.00017.
Values sent between devices are 32-bit elements; how exact they have to be, the bound alone decides.
No kernel may reach another device: no remote copies, remote signals or barrier semaphores. Data moves between devices by JAX's collectives and lax.ppermute only.
A program may use at most 64 MiB of HBM per device.

```python
import jax
import jax.numpy as jnp
from jax import lax

NODE_BOX = 128
BLOCK_PTS = 128
LSUB = 16
HB = 4
NBR = 8
FACES = 256
BOX_DEV = 64
BLK_DEV = 64
BOXES = 2048
CBLOCKS = 8192
N_VOL = 32
N_SURF = 4


def draw_block_list(key, part):
    devices = N_VOL * N_SURF
    count = BOX_DEV * LSUB
    keys = jax.random.split(jax.random.fold_in(key, 11), devices)

    def one_perm(single):
        return jax.random.permutation(single, devices)
    perms = jax.vmap(one_perm)(keys)
    owners = perms[:, jnp.arange(count) % devices]
    local = jax.random.randint(jax.random.fold_in(key, 12), (devices, count), 0, BLK_DEV)
    ident = owners * BLK_DEV + local
    ident = ident.reshape(N_VOL, N_SURF, BOX_DEV, LSUB)
    ident = jnp.transpose(ident, (1, 0, 2, 3)).reshape(N_SURF, N_VOL * BOX_DEV, LSUB)
    return ident.astype(jnp.int32)


def draw_neighbours(key, part):
    span = 2 * HB + 1
    scores = jax.random.randint(jax.random.fold_in(key, 21), (BOXES, span), 0, 1 << 20) * span
    scores = scores + jnp.arange(span)[None, :]
    order = jnp.argsort(scores, axis=1)[:, :NBR]
    ident = jnp.clip(jnp.arange(BOXES)[:, None] + order - HB, 0, BOXES - 1)
    return ident.astype(jnp.int32)


def place_ends(values, stream_key, smallest, largest):
    longest = values.shape.index(max(values.shape))
    spots = []
    for shift in (0, 1):
        where = [jax.random.randint(jax.random.fold_in(stream_key, axis), (), 0, length) for axis, length in enumerate(values.shape)]
        where[longest] = (where[longest] + shift) % values.shape[longest]
        spots.append(tuple(where))
    return values.at[spots[0]].set(smallest).at[spots[1]].set(largest)


def levels(key, extent, cuts, low, top_value):
    def one(axis_at, shards_of):
        heights = jax.random.uniform(jax.random.fold_in(jax.random.fold_in(key, 6), axis_at), (shards_of,), jnp.float32, low / len(cuts), top_value / len(cuts))
        return jnp.repeat(jnp.exp(heights), extent[axis_at] // shards_of).reshape((-1,) + (1,) * (len(extent) - axis_at - 1))

    level = one(*cuts[0])
    for cut in cuts[1:]:
        level = level * one(*cut)
    return level


def normal_values(own_key, dims, scale, limit, shards=(), kind=jnp.bfloat16):
    drawn = scale * jax.random.normal(own_key, dims, jnp.float32)
    if shards:
        drawn = drawn * levels(own_key, dims, shards, -0.22, 0.18)
    return jnp.clip(drawn, -limit, limit).astype(kind)


def setup_inputs(seed: int = 0) -> dict:
    splits = jax.random.split(jax.random.key(seed), 8)
    node_pos = normal_values(splits[0], (BOXES, 3, NODE_BOX), 1.0, 6.0, ((0, 32),), jnp.float32)
    centres = normal_values(splits[1], (CBLOCKS, 3, BLOCK_PTS), 1.0, 6.0, ((0, 128),), jnp.float32)
    coefs = normal_values(splits[2], (CBLOCKS, 3, BLOCK_PTS), 0.05, 0.3, ((0, 128),), jnp.float32)
    radii = jnp.clip(3.0 + 3.0 * jax.random.uniform(splits[3], (CBLOCKS, BLOCK_PTS), jnp.float32) ** levels(splits[3], (CBLOCKS, BLOCK_PTS), ((0, 128),), -0.2, 0.2), 3.0, 6.0)
    block_list = draw_block_list(jax.random.fold_in(splits[7], 71), 0)
    neighbours = draw_neighbours(jax.random.fold_in(splits[7], 71), 0)
    faces = place_ends(jax.random.randint(splits[6], (BOXES, 3, FACES), 0, NBR * NODE_BOX), jax.random.fold_in(splits[6], 1), 0, (NBR * NODE_BOX) - 1).astype(jnp.int32)
    return {"node_pos": node_pos, "centres": centres, "coefs": coefs, "radii": radii, "block_list": block_list, "neighbours": neighbours, "faces": faces}


def kernel_terms(nodes, centres, coefs, radii):
    diff = nodes[:, :, :, None] - centres[:, :, None, :]
    dist = jnp.sqrt(lax.optimization_barrier(jnp.sum(diff * diff, axis=1)))
    ratio = dist / radii[:, None, :]
    inside = jnp.maximum(1.0 - ratio, 0.0)
    weight = inside ** 4 * (4.0 * ratio + 1.0)
    return jnp.einsum('enp,ecp->ecn', weight, coefs, precision=lax.Precision.HIGHEST)

def blocked_terms(nodes, centres, coefs, radii):
    count = nodes.shape[0]

    def shaped(array):
        return array.reshape((count // 16, 16) + array.shape[1:])

    def one_group(group_args):
        return kernel_terms(group_args[0], group_args[1], group_args[2], group_args[3])
    out = lax.map(one_group, (shaped(nodes), shaped(centres), shaped(coefs), shaped(radii)))
    return out.reshape((count,) + out.shape[2:])

def swept_volume(corner_a, corner_b, corner_c):
    mid_a = corner_a[:, 0:3] + 0.5 * corner_a[:, 3:6]
    mid_b = corner_b[:, 0:3] + 0.5 * corner_b[:, 3:6]
    mid_c = corner_c[:, 0:3] + 0.5 * corner_c[:, 3:6]
    edge_u = mid_b - mid_a
    edge_w = mid_c - mid_a
    normal_x = 0.5 * (edge_u[:, 1] * edge_w[:, 2] - edge_u[:, 2] * edge_w[:, 1])
    normal_y = 0.5 * (edge_u[:, 2] * edge_w[:, 0] - edge_u[:, 0] * edge_w[:, 2])
    normal_z = 0.5 * (edge_u[:, 0] * edge_w[:, 1] - edge_u[:, 1] * edge_w[:, 0])
    motion = (corner_a[:, 3:6] + corner_b[:, 3:6] + corner_c[:, 3:6]) / 3.0
    return motion[:, 0] * normal_x + motion[:, 1] * normal_y + motion[:, 2] * normal_z

def reference(node_pos, centres, coefs, radii, block_list, neighbours, faces):
    entries = jnp.transpose(block_list, (1, 0, 2)).reshape(BOXES, N_SURF * LSUB)

    def one_box(box_args):
        nodes, ident = box_args
        count = ident.shape[0]
        spread = jnp.broadcast_to(nodes[None], (count,) + nodes.shape)
        terms = blocked_terms(spread, centres[ident], coefs[ident], radii[ident])
        return lax.optimization_barrier(jnp.sum(terms, axis=0))
    disp = lax.map(one_box, (node_pos, entries))
    velocity = disp / 0.5
    packed = jnp.concatenate([node_pos, disp], axis=1)
    beside_all = packed[neighbours]
    beside_all = jnp.moveaxis(beside_all, 1, 2).reshape(BOXES, 6, NBR * NODE_BOX)
    corner_a = jnp.take_along_axis(beside_all, faces[:, 0][:, None, :], axis=2)
    corner_b = jnp.take_along_axis(beside_all, faces[:, 1][:, None, :], axis=2)
    corner_c = jnp.take_along_axis(beside_all, faces[:, 2][:, None, :], axis=2)
    swept = swept_volume(corner_a, corner_b, corner_c)
    return (velocity, swept)
```

```python
import functools

import jax
import jax.numpy as jnp
from jax import lax
from jax.experimental import pallas as pl
from jax.experimental.pallas import tpu as pltpu
from jax.sharding import PartitionSpec as P

BF = jnp.bfloat16
F = jnp.float32
I = jnp.int32
BOTH = ("vol", "surf")
DEVICES = 128
SLOTS = 8
ROWS = 3 * SLOTS
BOX_DEV = 64
QUARTER = 16
TINY = 1e-30
VMEM = pl.BlockSpec(memory_space=pltpu.VMEM)
SMEM = pl.BlockSpec(memory_space=pltpu.SMEM)


def call(kernel, name, outs, ins, scratch=()):
    specs = [SMEM if space == "s" else VMEM for space, _ in ins]
    return pl.pallas_call(
        kernel,
        name=name,
        out_shape=outs,
        in_specs=specs,
        out_specs=tuple(VMEM for _ in outs),
        scratch_shapes=list(scratch),
    )(*[array for _, array in ins])


def split3(x):
    first = x.astype(BF).astype(F)
    rest = x - first
    second = rest.astype(BF).astype(F)
    return first, second, (rest - second).astype(BF).astype(F)


def slot_table(listed):
    owner = listed >> 6
    local = (listed & 63) + 1
    lanes = lax.broadcasted_iota(I, (BOX_DEV, DEVICES), 1)
    table = jnp.zeros((BOX_DEV, DEVICES), I)
    for k in range(listed.shape[1]):
        hit = owner[:, k : k + 1] == lanes
        table = jnp.where(hit, local[:, k : k + 1], table)
    table = table.astype(F)
    used = table > 0.0
    row = lax.broadcasted_iota(I, (BOX_DEV, BOX_DEV), 0)
    col = lax.broadcasted_iota(I, (BOX_DEV, BOX_DEV), 1)
    before = (col < row).astype(F).astype(BF)
    rank = jnp.dot(before, used.astype(F).astype(BF), preferred_element_type=F)
    return table, jnp.where(used, rank, -1.0)


def prep_kernel(list_ref, node_ref, send_ref, ids_ref):
    table, slot = slot_table(list_ref[...])
    slot_t = slot.T
    nodes = jnp.concatenate([node_ref[:, c, :] for c in range(3)], 1)
    parts = [p.astype(BF) for p in split3(nodes)]
    ids = []
    for j in range(SLOTS):
        ids.append(jnp.sum(jnp.where(slot == float(j), table - 1.0, 0.0), axis=0, keepdims=True))
        sel = (slot_t == float(j)).astype(F).astype(BF)
        got = sum(jnp.dot(sel, p, preferred_element_type=F) for p in parts)
        for c in range(3):
            send_ref[pl.ds(c * SLOTS + j, DEVICES, stride=ROWS), :] = got[:, c * 128 : (c + 1) * 128]
    stacked = jnp.concatenate(ids + [jnp.zeros((120, 128), F)], 0).T
    ids_ref[...] = stacked[:, 0:SLOTS].astype(I)


def feat_kernel(cen_ref, coef_ref, rad_ref, a_ref, cf_ref):
    def one(g, carry):
        c = cen_ref[g]
        r = rad_ref[pl.ds(g, 1), :]
        inv = 1.0 / (r * r)
        sq = c[0:1] * c[0:1] + c[1:2] * c[1:2] + c[2:3] * c[2:3]
        f = jnp.concatenate([c * (-2.0 * inv), inv, inv * sq, jnp.zeros((3, 128), F)], 0)
        p, q, t = split3(f)
        s = jnp.concatenate([p, p, p, q, q, t, jnp.zeros((80, 128), F)], 0)
        a_ref[pl.ds(pl.multiple_of(g * 128, 128), 128), :] = s.T.astype(BF)
        ks = split3(4.0 * coef_ref[g])
        z = jnp.concatenate([*ks, jnp.zeros((7, 128), F)], 0).astype(BF)
        cf_ref[pl.ds(pl.multiple_of(g * 16, 16), 16), :] = jnp.concatenate([z, z], 1)
        return carry

    lax.fori_loop(0, 64, one, 0)


def terms_kernel(ids_ref, x_ref, a_ref, cf_ref, o_ref, v_ref, q_ref, w_ref):
    def stage1(i, buf):
        base = pl.multiple_of(i * ROWS, ROWS)
        x = x_ref[pl.ds(base, 8), :]
        y = x_ref[pl.ds(base + 8, 8), :]
        z = x_ref[pl.ds(base + 16, 8), :]
        sq = x * x + y * y + z * z
        for f, value in enumerate((x, y, z, sq, jnp.ones_like(x))):
            for k, part in enumerate(split3(value)):
                v_ref[buf, k, pl.ds(f * 8, 8), :] = part
        for j in range(SLOTS):
            g = ids_ref[i, j]
            v = [v_ref[buf, k, pl.ds(j, 8, stride=8), :] for k in range(3)]
            b = jnp.concatenate([v[0], v[1], v[2], v[0], v[1], v[0], jnp.zeros((80, 128), F)], 0)
            a = a_ref[pl.ds(pl.multiple_of(g * 128, 128), 128), :]
            q_ref[buf, j] = jnp.dot(a, b.astype(BF), preferred_element_type=F)

    def stage2(buf):
        for j in range(SLOTS):
            m = jnp.maximum(q_ref[buf, j], TINY)
            q = m * lax.rsqrt(m)
            t = jnp.maximum(1.0 - q, 0.0)
            t = t * t
            w = (t * t) * (q + 0.25)
            high = w.astype(BF)
            w_ref[buf, j, 0:128, :] = high
            w_ref[buf, j, 128:256, :] = (w - high.astype(F)).astype(BF)

    def stage3(i, buf):
        base = pl.multiple_of(i * ROWS, ROWS)
        for j in range(SLOTS):
            g = ids_ref[i, j]
            c = cf_ref[pl.ds(pl.multiple_of(g * 16, 16), 16), :]
            r = jnp.dot(c, w_ref[buf, j], preferred_element_type=F)
            o_ref[pl.ds(base + j, 3, stride=8), :] = r[0:3] + r[3:6] + r[6:9]

    for k in range(3):
        for buf in range(2):
            v_ref[buf, k, pl.ds(40, 24), :] = jnp.zeros((24, 128), F)
    stage1(0, 0)
    stage1(1, 1)
    stage2(0)

    def two(h, carry):
        i = 2 * h
        stage1(i + 2, 0)
        stage2(1)
        stage3(i, 0)
        stage1(i + 3, 1)
        stage2(0)
        stage3(i + 1, 1)
        return carry

    lax.fori_loop(0, DEVICES // 2 - 1, two, 0)
    stage2(1)
    stage3(DEVICES - 2, 0)
    stage3(DEVICES - 1, 1)


def sum_kernel(where_ref, list_ref, back_ref, own_ref, one_ref, two_ref, three_ref, acc_ref):
    _, slot = slot_table(list_ref[...])
    acc = jnp.zeros((BOX_DEV, 384), F)
    for j in range(SLOTS):
        sel = (slot == float(j)).astype(F).astype(BF)
        terms = jnp.concatenate(
            [back_ref[pl.ds(c * SLOTS + j, DEVICES, stride=ROWS), :] for c in range(3)], 1
        )
        for part in split3(terms):
            acc = acc + jnp.dot(sel, part.astype(BF), preferred_element_type=F)
    for c in range(3):
        acc_ref[c] = acc[:, c * 128 : (c + 1) * 128]
    surf = where_ref[0]
    for k, ref in enumerate((own_ref, one_ref, two_ref, three_ref)):
        first = pl.multiple_of(((surf + k) & 3) * QUARTER, QUARTER)
        for c in range(3):
            ref[c * QUARTER : (c + 1) * QUARTER, :] = acc_ref[c, pl.ds(first, QUARTER), :]


def reduce_kernel(where_ref, node_ref, own_ref, one_ref, two_ref, three_ref, d_ref, up_ref, down_ref):
    d = own_ref[...] + one_ref[...] + two_ref[...] + three_ref[...]
    d_ref[...] = d
    first = pl.multiple_of(where_ref[0] * QUARTER, QUARTER)
    for c in range(3):
        x = node_ref[pl.ds(first, QUARTER), c, :]
        down_ref[c * 8 : c * 8 + 8, :] = x[0:8]
        up_ref[c * 8 : c * 8 + 8, :] = x[8:16]
        down_ref[24 + c * 8 : 32 + c * 8, :] = d[c * 16 : c * 16 + 8]
        up_ref[24 + c * 8 : 32 + c * 8, :] = d[c * 16 + 8 : c * 16 + 16]


def face_kernel(where_ref, near_ref, node_ref, d_ref, low_ref, high_ref, face_ref, o_ref, tab_ref, cor_ref):
    first = pl.multiple_of(where_ref[0] * QUARTER, QUARTER)
    origin = where_ref[1] * QUARTER - 8
    zero = jnp.zeros((32, 128), F)
    for c in range(8):
        if c < 3:
            own = node_ref[pl.ds(first, QUARTER), c, :]
        elif c < 6:
            own = d_ref[(c - 3) * 16 : (c - 2) * 16, :]
        if c < 6:
            rows = jnp.concatenate(
                [low_ref[c * 8 : c * 8 + 8, :], own, high_ref[c * 8 : c * 8 + 8, :]], 0
            )
        else:
            rows = zero
        tab_ref[pl.ds(c, 32, stride=8), :] = rows

    def one_box(b, carry):
        box = first + b
        tables = []
        for j in range(8):
            at = near_ref[box, j] - origin
            tables.append(tab_ref[pl.ds(pl.multiple_of(at * 8, 8), 8), :])
        for h in range(2):
            for k in range(3):
                code = face_ref[box, k : k + 1, h * 128 : (h + 1) * 128]
                code = jnp.broadcast_to(code, (8, 128))
                lane = code & 127
                which = code >> 7
                got = None
                for j in range(8):
                    value = jnp.take_along_axis(tables[j], lane, axis=1)
                    got = value if got is None else jnp.where(which == j, value, got)
                cor_ref[k, pl.ds(b * 2 + h, 8, stride=32), :] = got
        return carry

    lax.fori_loop(0, QUARTER, one_box, 0)

    def corner(k):
        part = [cor_ref[k, pl.ds(c * 32, 32), :] for c in range(6)]
        return [part[c] + 0.5 * part[c + 3] for c in range(3)], part[3:6]

    (ma, da), (mb, db), (mc, dc) = corner(0), corner(1), corner(2)
    u = [mb[c] - ma[c] for c in range(3)]
    w = [mc[c] - ma[c] for c in range(3)]
    swept = None
    for c in range(3):
        p, q = (c + 1) % 3, (c + 2) % 3
        normal = 0.5 * (u[p] * w[q] - u[q] * w[p])
        term = ((da[c] + db[c] + dc[c]) / 3.0) * normal
        swept = term if swept is None else swept + term
    o_ref[0:48, :] = d_ref[...] * 2.0
    o_ref[48:80, :] = swept


def out_kernel(where_ref, own_ref, one_ref, two_ref, three_ref, v_ref, s_ref):
    surf = where_ref[0]
    for k, ref in enumerate((own_ref, one_ref, two_ref, three_ref)):
        first = pl.multiple_of(((surf + 4 - k) & 3) * QUARTER, QUARTER)
        for c in range(3):
            v_ref[pl.ds(first, QUARTER), c, :] = ref[c * 16 : (c + 1) * 16, :]
        for h in range(2):
            s_ref[pl.ds(first, QUARTER), h * 128 : (h + 1) * 128] = ref[
                pl.ds(48 + h, QUARTER, stride=2), :
            ]


def to_all(array):
    return lax.all_to_all(array, BOTH, split_axis=0, concat_axis=0, tiled=True)


def around(arrays):
    return [
        lax.ppermute(a, "surf", [(i, (i + k) % 4) for i in range(4)])
        for k, a in zip((1, 2, 3), arrays)
    ]


def shape(*dims, kind=F):
    return jax.ShapeDtypeStruct(dims, kind)


def body(node_pos, centres, coefs, radii, block_list, neighbours, faces):
    listed = block_list[0]
    surf = lax.axis_index("surf")
    where = jnp.stack([surf, lax.axis_index("vol") * 4 + surf]).astype(I)
    send, ids = call(
        prep_kernel,
        "prep",
        (shape(DEVICES * ROWS, 128), shape(DEVICES, SLOTS, kind=I)),
        [("v", listed), ("v", node_pos)],
    )
    arrived = to_all(send.reshape(DEVICES, ROWS, 128)).reshape(DEVICES * ROWS, 128)
    asked = to_all(ids)
    table, weights = call(
        feat_kernel,
        "feats",
        (shape(64 * 128, 128, kind=BF), shape(64 * 16, 256, kind=BF)),
        [("v", centres), ("v", coefs), ("v", radii)],
    )
    (terms,) = call(
        terms_kernel,
        "terms",
        (shape(DEVICES * ROWS, 128),),
        [("s", asked), ("v", arrived), ("v", table), ("v", weights)],
        [
            pltpu.VMEM((2, 3, 64, 128), F),
            pltpu.VMEM((2, SLOTS, 128, 128), F),
            pltpu.VMEM((2, SLOTS, 256, 128), BF),
        ],
    )
    back = to_all(terms.reshape(DEVICES, ROWS, 128)).reshape(DEVICES * ROWS, 128)
    quarter = tuple(shape(48, 128) for _ in range(4))
    own, *rest = call(
        sum_kernel,
        "sums",
        quarter,
        [("s", where), ("v", listed), ("v", back)],
        [pltpu.VMEM((3, BOX_DEV, 128), F)],
    )
    d, up, down = call(
        reduce_kernel,
        "reduce",
        quarter[:3],
        [("s", where), ("v", node_pos), ("v", own)] + [("v", r) for r in around(rest)],
    )
    low = lax.ppermute(up, BOTH, [(i, i + 1) for i in range(DEVICES - 1)])
    high = lax.ppermute(down, BOTH, [(i + 1, i) for i in range(DEVICES - 1)])
    (mine,) = call(
        face_kernel,
        "faces",
        (shape(80, 128),),
        [("s", where), ("s", neighbours), ("v", node_pos), ("v", d), ("v", low), ("v", high), ("v", faces)],
        [pltpu.VMEM((256, 128), F), pltpu.VMEM((3, 256, 128), F)],
    )
    return tuple(
        call(
            out_kernel,
            "outs",
            (shape(BOX_DEV, 3, 128), shape(BOX_DEV, 256)),
            [("s", where), ("v", mine)] + [("v", r) for r in around([mine] * 3)],
        )
    )


def solution(mesh):
    placed = (
        P("vol", None, None),
        P(("vol", "surf"), None, None),
        P(("vol", "surf"), None, None),
        P(("vol", "surf"), None),
        P("surf", "vol", None),
        P("vol", None),
        P("vol", None, None),
    )
    return jax.shard_map(
        body,
        mesh=mesh,
        in_specs=placed,
        out_specs=(P("vol", None, None), P("vol", None)),
        check_vma=False,
    )
```

```python
import functools

import jax
import jax.numpy as jnp
from jax import lax
from jax.experimental import pallas as pl
from jax.experimental.pallas import tpu as pltpu
from jax.sharding import PartitionSpec as P

BF = jnp.bfloat16
F = jnp.float32
I = jnp.int32
BOTH = ("vol", "surf")
DEVICES = 128
SLOTS = 8
HALF = 4
ASK = 3 * HALF + 1
GIVE = 3 * HALF
BOX_DEV = 64
QUARTER = 16
HALO = 4
NEAR = QUARTER + 2 * HALO
TINY = 1e-30
VMEM = pl.BlockSpec(memory_space=pltpu.VMEM)
SMEM = pl.BlockSpec(memory_space=pltpu.SMEM)


def call(kernel, name, outs, ins, scratch=(), mib=8, us=2):
    specs = [SMEM if space == "s" else VMEM for space, _ in ins]
    return pl.pallas_call(
        kernel,
        name=name,
        out_shape=outs,
        in_specs=specs,
        out_specs=tuple(VMEM for _ in outs),
        scratch_shapes=list(scratch),
        compiler_params=pltpu.CompilerParams(vmem_limit_bytes=mib << 20),
        cost_estimate=pl.CostEstimate(flops=us * 10**9, bytes_accessed=us * 10**6, transcendentals=0),
    )(*[array for _, array in ins])


def split3(x):
    first = x.astype(BF).astype(F)
    rest = x - first
    second = rest.astype(BF).astype(F)
    return first, second, (rest - second).astype(BF).astype(F)


def slot_table(listed):
    listed = listed.astype(F).T.astype(I)
    owner = listed >> 6
    local = (listed & 63) + 1
    lanes = lax.broadcasted_iota(I, (BOX_DEV, DEVICES), 1)
    table = jnp.zeros((BOX_DEV, DEVICES), I)
    for k in range(listed.shape[1]):
        hit = owner[:, k : k + 1] == lanes
        table = jnp.where(hit, local[:, k : k + 1], table)
    table = table.astype(F)
    used = table > 0.0
    row = lax.broadcasted_iota(I, (BOX_DEV, BOX_DEV), 0)
    col = lax.broadcasted_iota(I, (BOX_DEV, BOX_DEV), 1)
    before = (col < row).astype(F).astype(BF)
    rank = jnp.dot(before, used.astype(F).astype(BF), preferred_element_type=F)
    return table, jnp.where(used, rank, -1.0)


def prep_kernel(list_ref, node_ref, low_ref, high_ref):
    table, slot = slot_table(list_ref[...])
    slot_t = slot.T
    nodes = jnp.concatenate([node_ref[c] for c in range(3)], 1)
    parts = [p.astype(BF) for p in split3(nodes)]
    for half, ref in enumerate((low_ref, high_ref)):
        ids = []
        for j in range(HALF):
            at = float(half * HALF + j)
            ids.append(jnp.sum(jnp.where(slot == at, table - 1.0, 0.0), axis=0, keepdims=True))
            sel = (slot_t == at).astype(F).astype(BF)
            got = sum(jnp.dot(sel, p, preferred_element_type=F) for p in parts)
            for c in range(3):
                ref[pl.ds(c * HALF + j, DEVICES, stride=ASK), :] = got[:, c * 128 : (c + 1) * 128]
        stacked = jnp.concatenate(ids + [jnp.zeros((128 - HALF, 128), F)], 0).T
        ref[pl.ds(ASK - 1, DEVICES, stride=ASK), :] = stacked


def feat_kernel(cen_ref, coef_ref, rad_ref, a_ref, cf_ref):
    def one(g, carry):
        c = cen_ref[:, pl.ds(g, 1), :].reshape(3, 128)
        r = rad_ref[pl.ds(g, 1), :]
        inv = 1.0 / (r * r)
        sq = c[0:1] * c[0:1] + c[1:2] * c[1:2] + c[2:3] * c[2:3]
        f = jnp.concatenate([c * (-2.0 * inv), inv, inv * sq, jnp.zeros((3, 128), F)], 0)
        p, q, t = split3(f)
        s = jnp.concatenate([p, p, p, q, q, t, jnp.zeros((80, 128), F)], 0)
        a_ref[pl.ds(pl.multiple_of(g * 128, 128), 128), :] = s.T.astype(BF)
        ks = split3(4.0 * coef_ref[:, pl.ds(g, 1), :].reshape(3, 128))
        z = jnp.concatenate([*ks, jnp.zeros((7, 128), F)], 0).astype(BF)
        cf_ref[pl.ds(pl.multiple_of(g * 16, 16), 16), :] = jnp.concatenate([z, z], 1)
        return carry

    lax.fori_loop(0, 64, one, 0)


def terms_kernel(x_ref, a_ref, cf_ref, o_ref, v_ref, q_ref, w_ref, stage_ref, ids_ref, sem):
    stage_ref[...] = x_ref[pl.ds(ASK - 1, DEVICES, stride=ASK), :].T[0:8].astype(I)
    copy = pltpu.make_async_copy(stage_ref, ids_ref, sem)
    copy.start()
    for k in range(3):
        for buf in range(2):
            v_ref[buf, k, pl.ds(40, 24), :] = jnp.zeros((24, 128), F)
    copy.wait()

    def number(i, e):
        return ids_ref[e % HALF, 2 * i + e // HALF]

    def stage1(i, buf):
        base = i * (2 * ASK)
        x, y, z = [
            jnp.concatenate(
                [x_ref[pl.ds(base + p * ASK + c * HALF, HALF), :] for p in range(2)], 0
            )
            for c in range(3)
        ]
        sq = x * x + y * y + z * z
        for f, value in enumerate((x, y, z, sq, jnp.ones_like(x))):
            for k, part in enumerate(split3(value)):
                v_ref[buf, k, pl.ds(f * 8, 8), :] = part
        for e in range(8):
            g = number(i, e)
            v = [v_ref[buf, k, pl.ds(e, 8, stride=8), :] for k in range(3)]
            b = jnp.concatenate([v[0], v[1], v[2], v[0], v[1], v[0], jnp.zeros((80, 128), F)], 0)
            a = a_ref[pl.ds(pl.multiple_of(g * 128, 128), 128), :]
            q_ref[buf, e] = jnp.dot(a, b.astype(BF), preferred_element_type=F)

    def stage2(buf):
        for e in range(8):
            m = jnp.maximum(q_ref[buf, e], TINY)
            q = m * lax.rsqrt(m)
            t = jnp.maximum(1.0 - q, 0.0)
            t = t * t
            w = (t * t) * (q + 0.25)
            high = w.astype(BF)
            w_ref[buf, e, 0:128, :] = high
            w_ref[buf, e, 128:256, :] = (w - high.astype(F)).astype(BF)

    def stage3(i, buf):
        base = pl.multiple_of(i * (2 * GIVE), 2 * GIVE)
        for e in range(8):
            g = number(i, e)
            c = cf_ref[pl.ds(pl.multiple_of(g * 16, 16), 16), :]
            r = jnp.dot(c, w_ref[buf, e], preferred_element_type=F)
            row = (e // HALF) * GIVE + e % HALF
            o_ref[pl.ds(base + row, 3, stride=HALF), :] = r[0:3] + r[3:6] + r[6:9]

    groups = DEVICES // 2
    stage1(0, 0)
    stage1(1, 1)
    stage2(0)

    def two(h, carry):
        i = 2 * h
        stage1(i + 2, 0)
        stage2(1)
        stage3(i, 0)
        stage1(i + 3, 1)
        stage2(0)
        stage3(i + 1, 1)
        return carry

    lax.fori_loop(0, groups // 2 - 1, two, 0)
    stage2(1)
    stage3(groups - 2, 0)
    stage3(groups - 1, 1)


def sum_kernel(where_ref, list_ref, node_ref, low_ref, high_ref, *refs):
    quarters, edges, acc_ref = refs[0:4], refs[4:8], refs[8]
    _, slot = slot_table(list_ref[...])
    acc = jnp.zeros((BOX_DEV, 384), F)
    for j in range(SLOTS):
        ref = (low_ref, high_ref)[j // HALF]
        sel = (slot == float(j)).astype(F).astype(BF)
        terms = jnp.concatenate(
            [ref[pl.ds(c * HALF + j % HALF, DEVICES, stride=GIVE), :] for c in range(3)], 1
        )
        for part in split3(terms):
            acc = acc + jnp.dot(sel, part.astype(BF), preferred_element_type=F)
    for c in range(3):
        acc_ref[c, 0:8, :] = jnp.zeros((8, 128), F)
        acc_ref[c, 64:72, :] = jnp.zeros((8, 128), F)
        acc_ref[c, HALO : HALO + BOX_DEV, :] = acc[:, c * 128 : (c + 1) * 128]
    surf = where_ref[0]
    for k, ref in enumerate(quarters):
        first = pl.multiple_of(((surf + k) & 3) * QUARTER, QUARTER)
        for c in range(3):
            ref[c * NEAR : (c + 1) * NEAR, :] = acc_ref[c, pl.ds(first, NEAR), :]
    zero = jnp.zeros((HALO, 128), F)
    d = [acc[:, c * 128 : (c + 1) * 128] for c in range(3)]
    x = [node_ref[c] for c in range(3)]
    head = jnp.concatenate([t[0:HALO] for t in d] + [zero] + [t[0:HALO] for t in x] + [zero], 0)
    tail = jnp.concatenate([t[60:64] for t in d] + [zero] + [t[60:64] for t in x] + [zero], 0)
    for k, ref in enumerate(edges):
        pick = jnp.where(surf == k, 1.0, 0.0)
        both = pick * tail + (1.0 - pick) * head
        ref[...] = both if k == 0 else both[0:16]


def face_kernel(where_ref, near_ref, node_ref, *refs):
    quarters, edges = refs[0:4], refs[4:8]
    face_ref, o_ref, tab_ref, cor_ref, x_ref, code_ref = refs[8:]
    surf = where_ref[0]
    first = pl.multiple_of(surf * QUARTER, QUARTER)
    origin = where_ref[1] * QUARTER - HALO
    is_low = jnp.where(surf == 0, 1.0, 0.0)
    is_high = jnp.where(surf == 3, 1.0, 0.0)
    d = quarters[0][...] + quarters[1][...] + quarters[2][...] + quarters[3][...]
    edge_d = edges[0][0:16] + edges[1][...] + edges[2][...] + edges[3][...]
    edge_x = edges[0][16:32]
    zero = jnp.zeros((QUARTER, 128), F)

    def placed(c, edge):
        part = edge[c * HALO : (c + 1) * HALO]
        return jnp.concatenate([is_low * part, zero, is_high * part], 0)

    mine = []
    for c in range(3):
        x_ref[c, 0:8, :] = jnp.zeros((8, 128), F)
        x_ref[c, 64:72, :] = jnp.zeros((8, 128), F)
        x_ref[c, HALO : HALO + BOX_DEV, :] = node_ref[c]
        disp = d[c * NEAR : (c + 1) * NEAR] + placed(c, edge_d)
        mine.append(disp[HALO : HALO + QUARTER])
        tab_ref[pl.ds(c, NEAR, stride=8), :] = x_ref[c, pl.ds(first, NEAR), :] + placed(c, edge_x)
        tab_ref[pl.ds(c + 3, NEAR, stride=8), :] = disp
    for c in (6, 7):
        tab_ref[pl.ds(c, NEAR, stride=8), :] = jnp.zeros((NEAR, 128), F)

    for k in range(3):
        for h in range(2):
            code_ref[pl.ds((k * 2 + h) * QUARTER, QUARTER), :] = face_ref[
                k, pl.ds(first, QUARTER), h * 128 : (h + 1) * 128
            ]

    def one_box(b, carry):
        box = first + b
        tables = []
        for j in range(8):
            at = near_ref[j, box] - origin
            tables.append(tab_ref[pl.ds(pl.multiple_of(at * 8, 8), 8), :])
        for h in range(2):
            for k in range(3):
                code = code_ref[pl.ds((k * 2 + h) * QUARTER + b, 1), :]
                code = jnp.broadcast_to(code, (8, 128))
                lane = code & 127
                which = code >> 7
                got = None
                for j in range(8):
                    value = jnp.take_along_axis(tables[j], lane, axis=1)
                    got = value if got is None else jnp.where(which == j, value, got)
                cor_ref[k, pl.ds(b * 2 + h, 8, stride=32), :] = got
        return carry

    lax.fori_loop(0, QUARTER, one_box, 0)

    def corner(k):
        part = [cor_ref[k, pl.ds(c * 32, 32), :] for c in range(6)]
        return [part[c] + 0.5 * part[c + 3] for c in range(3)], part[3:6]

    (ma, da), (mb, db), (mc, dc) = corner(0), corner(1), corner(2)
    u = [mb[c] - ma[c] for c in range(3)]
    w = [mc[c] - ma[c] for c in range(3)]
    swept = None
    for c in range(3):
        p, q = (c + 1) % 3, (c + 2) % 3
        normal = 0.5 * (u[p] * w[q] - u[q] * w[p])
        term = ((da[c] + db[c] + dc[c]) / 3.0) * normal
        swept = term if swept is None else swept + term
    for c in range(3):
        o_ref[c * 16 : (c + 1) * 16, :] = mine[c] * 2.0
    o_ref[48:80, :] = swept


def out_kernel(where_ref, own_ref, one_ref, two_ref, three_ref, v_ref, s_ref):
    surf = where_ref[0]
    for k, ref in enumerate((own_ref, one_ref, two_ref, three_ref)):
        first = pl.multiple_of(((surf + 4 - k) & 3) * QUARTER, QUARTER)
        for c in range(3):
            v_ref[c, pl.ds(first, QUARTER), :] = ref[c * 16 : (c + 1) * 16, :]
        for h in range(2):
            s_ref[pl.ds(first, QUARTER), h * 128 : (h + 1) * 128] = ref[
                pl.ds(48 + h, QUARTER, stride=2), :
            ]


def to_all(array):
    rows = array.shape[0] // DEVICES
    packets = array.reshape(DEVICES, rows, 1, 128)
    packets = lax.all_to_all(packets, BOTH, split_axis=0, concat_axis=0, tiled=True)
    return packets.reshape(DEVICES * rows, 128)


def around(arrays):
    return [
        lax.ppermute(a, "surf", [(i, (i + k) % 4) for i in range(4)])
        for k, a in zip((1, 2, 3), arrays)
    ]


def edge_pairs(k):
    up = [(v * 4 + k, (v + 1) * 4) for v in range(31)]
    down = [((v + 1) * 4 + (k + 1) % 4, v * 4 + 3) for v in range(31)]
    return up + down


def shape(*dims, kind=F):
    return jax.ShapeDtypeStruct(dims, kind)


def body(node_pos, centres, coefs, radii, block_list, neighbours, faces):
    listed = block_list[0].T
    nodes, cens, weights = [a.transpose(1, 0, 2) for a in (node_pos, centres, coefs)]
    surf = lax.axis_index("surf")
    where = jnp.stack([surf, lax.axis_index("vol") * 4 + surf]).astype(I)
    sent = call(
        prep_kernel,
        "prep",
        (shape(DEVICES * ASK, 128),) * 2,
        [("v", listed), ("v", nodes)],
    )
    tables = call(
        feat_kernel,
        "feats",
        (shape(64 * 128, 128, kind=BF), shape(64 * 16, 256, kind=BF)),
        [("v", cens), ("v", weights), ("v", radii)],
        us=10,
    )
    back = []
    for packet in sent:
        (terms,) = call(
            terms_kernel,
            "terms",
            (shape(DEVICES * GIVE, 128),),
            [("v", to_all(packet)), ("v", tables[0]), ("v", tables[1])],
            [
                pltpu.VMEM((2, 3, 64, 128), F),
                pltpu.VMEM((2, 8, 128, 128), F),
                pltpu.VMEM((2, 8, 256, 128), BF),
                pltpu.VMEM((8, 128), I),
                pltpu.SMEM((8, 128), I),
                pltpu.SemaphoreType.DMA,
            ],
            mib=16,
            us=30,
        )
        back.append(to_all(terms))
    own = call(
        sum_kernel,
        "sums",
        (shape(3 * NEAR, 128),) * 4 + (shape(32, 128),) + (shape(16, 128),) * 3,
        [("s", where), ("v", listed), ("v", nodes), ("v", back[0]), ("v", back[1])],
        [pltpu.VMEM((3, 72, 128), F)],
    )
    quarters = [own[0], *around(own[1:4])]
    edges = [lax.ppermute(own[4 + k], BOTH, edge_pairs(k)) for k in range(4)]
    (mine,) = call(
        face_kernel,
        "faces",
        (shape(80, 128),),
        [("s", where), ("s", neighbours.T), ("v", nodes)]
        + [("v", a) for a in quarters + edges]
        + [("v", faces.transpose(1, 0, 2))],
        [
            pltpu.VMEM((8 * NEAR, 128), F),
            pltpu.VMEM((3, 256, 128), F),
            pltpu.VMEM((3, 72, 128), F),
            pltpu.VMEM((96, 128), I),
        ],
    )
    velocity, swept = call(
        out_kernel,
        "outs",
        (shape(3, BOX_DEV, 128), shape(BOX_DEV, 256)),
        [("s", where), ("v", mine)] + [("v", r) for r in around([mine] * 3)],
    )
    return velocity.transpose(1, 0, 2), swept


def solution(mesh):
    placed = (
        P("vol", None, None),
        P(("vol", "surf"), None, None),
        P(("vol", "surf"), None, None),
        P(("vol", "surf"), None),
        P("surf", "vol", None),
        P("vol", None),
        P("vol", None, None),
    )
    return jax.shard_map(
        body,
        mesh=mesh,
        in_specs=placed,
        out_specs=(P("vol", None, None), P("vol", None)),
        check_vma=False,
    )
```

```python
import functools

import jax
import jax.numpy as jnp
from jax import lax
from jax.experimental import pallas as pl
from jax.experimental.pallas import tpu as pltpu
from jax.sharding import PartitionSpec as P

BF = jnp.bfloat16
F = jnp.float32
I = jnp.int32
BOTH = ("vol", "surf")
DEVICES = 128
SLOTS = 8
ASK = 3 * SLOTS + 1
GIVE = 3 * SLOTS
UNROLL = 8
BOX_DEV = 64
QUARTER = 16
HALO = 4
NEAR = QUARTER + 2 * HALO
TINY = 1e-30
VMEM = pl.BlockSpec(memory_space=pltpu.VMEM)
SMEM = pl.BlockSpec(memory_space=pltpu.SMEM)


def call(kernel, name, outs, ins, scratch=(), mib=8, us=2):
    specs = [SMEM if space == "s" else VMEM for space, _ in ins]
    return pl.pallas_call(
        kernel,
        name=name,
        out_shape=outs,
        in_specs=specs,
        out_specs=tuple(VMEM for _ in outs),
        scratch_shapes=list(scratch),
        compiler_params=pltpu.CompilerParams(vmem_limit_bytes=mib << 20),
        cost_estimate=pl.CostEstimate(flops=us * 10**9, bytes_accessed=us * 10**6, transcendentals=0),
    )(*[array for _, array in ins])


def split3(x):
    first = x.astype(BF).astype(F)
    rest = x - first
    second = rest.astype(BF).astype(F)
    return first, second, (rest - second).astype(BF).astype(F)


def slot_table(listed):
    listed = listed.astype(F).T.astype(I)
    owner = listed >> 6
    local = (listed & 63) + 1
    lanes = lax.broadcasted_iota(I, (BOX_DEV, DEVICES), 1)
    table = jnp.zeros((BOX_DEV, DEVICES), I)
    for k in range(listed.shape[1]):
        hit = owner[:, k : k + 1] == lanes
        table = jnp.where(hit, local[:, k : k + 1], table)
    table = table.astype(F)
    used = table > 0.0
    row = lax.broadcasted_iota(I, (BOX_DEV, BOX_DEV), 0)
    col = lax.broadcasted_iota(I, (BOX_DEV, BOX_DEV), 1)
    before = (col < row).astype(F).astype(BF)
    rank = jnp.dot(before, used.astype(F).astype(BF), preferred_element_type=F)
    return table, jnp.where(used, rank, -1.0)


def prep_kernel(list_ref, node_ref, o_ref):
    table, slot = slot_table(list_ref[...])
    slot_t = slot.T
    nodes = jnp.concatenate([node_ref[c] for c in range(3)], 1)
    parts = [p.astype(BF) for p in split3(nodes)]
    ids = []
    for j in range(SLOTS):
        at = float(j)
        ids.append(jnp.sum(jnp.where(slot == at, table - 1.0, 0.0), axis=0, keepdims=True))
        sel = (slot_t == at).astype(F).astype(BF)
        got = sum(jnp.dot(sel, p, preferred_element_type=F) for p in parts)
        for c in range(3):
            o_ref[pl.ds(c * SLOTS + j, DEVICES, stride=ASK), :] = got[:, c * 128 : (c + 1) * 128]
    stacked = jnp.concatenate(ids + [jnp.zeros((128 - SLOTS, 128), F)], 0).T
    o_ref[pl.ds(ASK - 1, DEVICES, stride=ASK), :] = stacked


def feat_kernel(cen_ref, coef_ref, rad_ref, a_ref, cf_ref):
    def one(g, carry):
        c = cen_ref[:, pl.ds(g, 1), :].reshape(3, 128)
        r = rad_ref[pl.ds(g, 1), :]
        inv = 1.0 / (r * r)
        sq = c[0:1] * c[0:1] + c[1:2] * c[1:2] + c[2:3] * c[2:3]
        f = jnp.concatenate([c * (-2.0 * inv), inv, inv * sq, jnp.zeros((3, 128), F)], 0)
        p, q, t = split3(f)
        s = jnp.concatenate([p, p, p, q, q, t, jnp.zeros((80, 128), F)], 0)
        a_ref[pl.ds(pl.multiple_of(g * 128, 128), 128), :] = s.T.astype(BF)
        ks = split3(4.0 * coef_ref[:, pl.ds(g, 1), :].reshape(3, 128))
        z = jnp.concatenate([*ks, jnp.zeros((7, 128), F)], 0).astype(BF)
        cf_ref[pl.ds(pl.multiple_of(g * 16, 16), 16), :] = jnp.concatenate([z, z], 1)
        return carry

    lax.fori_loop(0, 64, one, 0)


def terms_kernel(x_ref, a_ref, cf_ref, o_ref, v_ref, b_ref, q_ref, w_ref, stage_ref, ids_ref, sem):
    stage_ref[...] = x_ref[pl.ds(ASK - 1, DEVICES, stride=ASK), :].T[0:SLOTS].astype(I)
    copy = pltpu.make_async_copy(stage_ref, ids_ref, sem)
    copy.start()
    for buf in range(2):
        for j in range(SLOTS):
            b_ref[buf, j, 48:128, :] = jnp.zeros((80, 128), BF)
        for k in range(3):
            v_ref[buf, k, pl.ds(32, 32), :] = jnp.zeros((32, 128), F)
        v_ref[buf, 0, pl.ds(32, 8), :] = jnp.ones((8, 128), F)
    copy.wait()

    def stage0(i, buf):
        base = jnp.minimum(i, DEVICES - 1) * ASK
        x, y, z = [x_ref[pl.ds(base + c * SLOTS, SLOTS), :] for c in range(3)]
        for f, value in enumerate((x, y, z, x * x + y * y + z * z)):
            first = value.astype(BF).astype(F)
            rest = value - first
            second = rest.astype(BF).astype(F)
            for k, part in enumerate((first, second, rest - second)):
                v_ref[buf, k, pl.ds(f * 8, 8), :] = part
        for j in range(SLOTS):
            v = [v_ref[buf, k, pl.ds(j, 8, stride=8), :] for k in range(3)]
            b_ref[buf, j, 0:48, :] = jnp.concatenate(
                [v[0], v[1], v[2], v[0], v[1], v[0]], 0
            ).astype(BF)

    def stage1(i, buf, j):
        g = ids_ref[j, jnp.minimum(i, DEVICES - 1)]
        a = a_ref[pl.ds(pl.multiple_of(g * 128, 128), 128), :]
        q_ref[buf, j] = jnp.dot(a, b_ref[buf, j], preferred_element_type=F)

    def stage2(buf, j):
        m = jnp.maximum(q_ref[buf, j], TINY)
        q = m * lax.rsqrt(m)
        t = jnp.maximum(1.0 - q, 0.0)
        t = t * t
        w = (t * t) * (q + 0.25)
        high = w.astype(BF)
        w_ref[buf, j, 0:128, :] = high
        w_ref[buf, j, 128:256, :] = (w - high.astype(F)).astype(BF)

    def stage3(i, buf, j):
        base = pl.multiple_of(i * GIVE, GIVE)
        g = ids_ref[j, i]
        c = cf_ref[pl.ds(pl.multiple_of(g * 16, 16), 16), :]
        r = jnp.dot(c, w_ref[buf, j], preferred_element_type=F)
        o_ref[pl.ds(base + j, 3, stride=SLOTS), :] = r[0:3] + r[3:6] + r[6:9]

    slots = range(SLOTS)
    stage0(0, 0)
    stage0(1, 1)
    for j in slots:
        stage1(0, 0, j)
    stage0(2, 0)
    for j in slots:
        stage1(1, 1, j)
    for j in slots:
        stage2(0, j)

    def some(h, carry):
        for u in range(UNROLL):
            i = h * UNROLL + u
            buf = u % 2
            for j in slots:
                stage1(i + 2, buf, j)
                stage2(1 - buf, j)
                stage3(i, buf, j)
            stage0(i + 3, 1 - buf)
        return carry

    lax.fori_loop(0, DEVICES // UNROLL, some, 0)


def sum_kernel(where_ref, list_ref, node_ref, back_ref, *refs):
    quarters, edges, acc_ref = refs[0:4], refs[4:8], refs[8]
    _, slot = slot_table(list_ref[...])
    acc = jnp.zeros((BOX_DEV, 384), F)
    for j in range(SLOTS):
        sel = (slot == float(j)).astype(F).astype(BF)
        terms = jnp.concatenate(
            [back_ref[pl.ds(c * SLOTS + j, DEVICES, stride=GIVE), :] for c in range(3)], 1
        )
        for part in split3(terms):
            acc = acc + jnp.dot(sel, part.astype(BF), preferred_element_type=F)
    for c in range(3):
        acc_ref[c, 0:8, :] = jnp.zeros((8, 128), F)
        acc_ref[c, 64:72, :] = jnp.zeros((8, 128), F)
        acc_ref[c, HALO : HALO + BOX_DEV, :] = acc[:, c * 128 : (c + 1) * 128]
    surf = where_ref[0]
    for k, ref in enumerate(quarters):
        first = pl.multiple_of(((surf + k) & 3) * QUARTER, QUARTER)
        for c in range(3):
            ref[c * NEAR : (c + 1) * NEAR, :] = acc_ref[c, pl.ds(first, NEAR), :]
    zero = jnp.zeros((HALO, 128), F)
    d = [acc[:, c * 128 : (c + 1) * 128] for c in range(3)]
    x = [node_ref[c] for c in range(3)]
    head = jnp.concatenate([t[0:HALO] for t in d] + [zero] + [t[0:HALO] for t in x] + [zero], 0)
    tail = jnp.concatenate([t[60:64] for t in d] + [zero] + [t[60:64] for t in x] + [zero], 0)
    for k, ref in enumerate(edges):
        pick = jnp.where(surf == k, 1.0, 0.0)
        both = pick * tail + (1.0 - pick) * head
        ref[...] = both if k == 0 else both[0:16]


def face_kernel(where_ref, near_ref, node_ref, *refs):
    quarters, edges = refs[0:4], refs[4:8]
    face_ref, o_ref, tab_ref, cor_ref, x_ref, code_ref = refs[8:]
    surf = where_ref[0]
    first = pl.multiple_of(surf * QUARTER, QUARTER)
    origin = where_ref[1] * QUARTER - HALO
    is_low = jnp.where(surf == 0, 1.0, 0.0)
    is_high = jnp.where(surf == 3, 1.0, 0.0)
    d = quarters[0][...] + quarters[1][...] + quarters[2][...] + quarters[3][...]
    edge_d = edges[0][0:16] + edges[1][...] + edges[2][...] + edges[3][...]
    edge_x = edges[0][16:32]
    zero = jnp.zeros((QUARTER, 128), F)

    def placed(c, edge):
        part = edge[c * HALO : (c + 1) * HALO]
        return jnp.concatenate([is_low * part, zero, is_high * part], 0)

    mine = []
    for c in range(3):
        x_ref[c, 0:8, :] = jnp.zeros((8, 128), F)
        x_ref[c, 64:72, :] = jnp.zeros((8, 128), F)
        x_ref[c, HALO : HALO + BOX_DEV, :] = node_ref[c]
        disp = d[c * NEAR : (c + 1) * NEAR] + placed(c, edge_d)
        mine.append(disp[HALO : HALO + QUARTER])
        tab_ref[pl.ds(c, NEAR, stride=8), :] = x_ref[c, pl.ds(first, NEAR), :] + placed(c, edge_x)
        tab_ref[pl.ds(c + 3, NEAR, stride=8), :] = disp
    for c in (6, 7):
        tab_ref[pl.ds(c, NEAR, stride=8), :] = jnp.zeros((NEAR, 128), F)

    for k in range(3):
        for h in range(2):
            code_ref[pl.ds((k * 2 + h) * QUARTER, QUARTER), :] = face_ref[
                k, pl.ds(first, QUARTER), h * 128 : (h + 1) * 128
            ]

    def one_box(b, carry):
        box = first + b
        tables = []
        for j in range(8):
            at = near_ref[j, box] - origin
            tables.append(tab_ref[pl.ds(pl.multiple_of(at * 8, 8), 8), :])
        for h in range(2):
            for k in range(3):
                code = code_ref[pl.ds((k * 2 + h) * QUARTER + b, 1), :]
                code = jnp.broadcast_to(code, (8, 128))
                lane = code & 127
                which = code >> 7
                got = None
                for j in range(8):
                    value = jnp.take_along_axis(tables[j], lane, axis=1)
                    got = value if got is None else jnp.where(which == j, value, got)
                cor_ref[k, pl.ds(b * 2 + h, 8, stride=32), :] = got
        return carry

    lax.fori_loop(0, QUARTER, one_box, 0)

    def corner(k):
        part = [cor_ref[k, pl.ds(c * 32, 32), :] for c in range(6)]
        return [part[c] + 0.5 * part[c + 3] for c in range(3)], part[3:6]

    (ma, da), (mb, db), (mc, dc) = corner(0), corner(1), corner(2)
    u = [mb[c] - ma[c] for c in range(3)]
    w = [mc[c] - ma[c] for c in range(3)]
    swept = None
    for c in range(3):
        p, q = (c + 1) % 3, (c + 2) % 3
        normal = 0.5 * (u[p] * w[q] - u[q] * w[p])
        term = ((da[c] + db[c] + dc[c]) / 3.0) * normal
        swept = term if swept is None else swept + term
    for c in range(3):
        o_ref[c * 16 : (c + 1) * 16, :] = mine[c] * 2.0
    o_ref[48:80, :] = swept


def out_kernel(where_ref, own_ref, one_ref, two_ref, three_ref, v_ref, s_ref):
    surf = where_ref[0]
    for k, ref in enumerate((own_ref, one_ref, two_ref, three_ref)):
        first = pl.multiple_of(((surf + 4 - k) & 3) * QUARTER, QUARTER)
        for c in range(3):
            v_ref[c, pl.ds(first, QUARTER), :] = ref[c * 16 : (c + 1) * 16, :]
        for h in range(2):
            s_ref[pl.ds(first, QUARTER), h * 128 : (h + 1) * 128] = ref[
                pl.ds(48 + h, QUARTER, stride=2), :
            ]


def to_all(array):
    rows = array.shape[0] // DEVICES
    packets = array.reshape(DEVICES, rows, 1, 128)
    packets = lax.all_to_all(packets, BOTH, split_axis=0, concat_axis=0, tiled=True)
    return packets.reshape(DEVICES * rows, 128)


def around(arrays):
    return [
        lax.ppermute(a, "surf", [(i, (i + k) % 4) for i in range(4)])
        for k, a in zip((1, 2, 3), arrays)
    ]


def edge_pairs(k):
    up = [(v * 4 + k, (v + 1) * 4) for v in range(31)]
    down = [((v + 1) * 4 + (k + 1) % 4, v * 4 + 3) for v in range(31)]
    return up + down


def shape(*dims, kind=F):
    return jax.ShapeDtypeStruct(dims, kind)


def body(node_pos, centres, coefs, radii, block_list, neighbours, faces):
    listed = block_list[0].T
    nodes, cens, weights = [a.transpose(1, 0, 2) for a in (node_pos, centres, coefs)]
    surf = lax.axis_index("surf")
    where = jnp.stack([surf, lax.axis_index("vol") * 4 + surf]).astype(I)
    (sent,) = call(
        prep_kernel,
        "prep",
        (shape(DEVICES * ASK, 128),),
        [("v", listed), ("v", nodes)],
    )
    tables = call(
        feat_kernel,
        "feats",
        (shape(64 * 128, 128, kind=BF), shape(64 * 16, 256, kind=BF)),
        [("v", cens), ("v", weights), ("v", radii)],
        us=10,
    )
    (terms,) = call(
        terms_kernel,
        "terms",
        (shape(DEVICES * GIVE, 128),),
        [("v", to_all(sent)), ("v", tables[0]), ("v", tables[1])],
        [
            pltpu.VMEM((2, 3, 64, 128), F),
            pltpu.VMEM((2, SLOTS, 128, 128), BF),
            pltpu.VMEM((2, SLOTS, 128, 128), F),
            pltpu.VMEM((2, SLOTS, 256, 128), BF),
            pltpu.VMEM((SLOTS, 128), I),
            pltpu.SMEM((SLOTS, 128), I),
            pltpu.SemaphoreType.DMA,
        ],
        mib=16,
        us=45,
    )
    own = call(
        sum_kernel,
        "sums",
        (shape(3 * NEAR, 128),) * 4 + (shape(32, 128),) + (shape(16, 128),) * 3,
        [("s", where), ("v", listed), ("v", nodes), ("v", to_all(terms))],
        [pltpu.VMEM((3, 72, 128), F)],
    )
    quarters = [own[0], *around(own[1:4])]
    edges = [lax.ppermute(own[4 + k], BOTH, edge_pairs(k)) for k in range(4)]
    (mine,) = call(
        face_kernel,
        "faces",
        (shape(80, 128),),
        [("s", where), ("s", neighbours.T), ("v", nodes)]
        + [("v", a) for a in quarters + edges]
        + [("v", faces.transpose(1, 0, 2))],
        [
            pltpu.VMEM((8 * NEAR, 128), F),
            pltpu.VMEM((3, 256, 128), F),
            pltpu.VMEM((3, 72, 128), F),
            pltpu.VMEM((96, 128), I),
        ],
    )
    velocity, swept = call(
        out_kernel,
        "outs",
        (shape(3, BOX_DEV, 128), shape(BOX_DEV, 256)),
        [("s", where), ("v", mine)] + [("v", r) for r in around([mine] * 3)],
    )
    return velocity.transpose(1, 0, 2), swept


def solution(mesh):
    placed = (
        P("vol", None, None),
        P(("vol", "surf"), None, None),
        P(("vol", "surf"), None, None),
        P(("vol", "surf"), None),
        P("surf", "vol", None),
        P("vol", None),
        P("vol", None, None),
    )
    return jax.shard_map(
        body,
        mesh=mesh,
        in_specs=placed,
        out_specs=(P("vol", None, None), P("vol", None)),
        check_vma=False,
    )
```

```python
import functools

import jax
import jax.numpy as jnp
from jax import lax
from jax.experimental import pallas as pl
from jax.experimental.pallas import tpu as pltpu
from jax.sharding import PartitionSpec as P

BF = jnp.bfloat16
F = jnp.float32
I = jnp.int32
BOTH = ("vol", "surf")
DEVICES = 128
SLOTS = 8
ASK = 3 * SLOTS + 1
GIVE = 3 * SLOTS
UNROLL = 8
BOX_DEV = 64
HALO = 4
NEAR = BOX_DEV + 2 * HALO
TINY = 1e-30
VMEM = pl.BlockSpec(memory_space=pltpu.VMEM)
SMEM = pl.BlockSpec(memory_space=pltpu.SMEM)


def call(kernel, name, outs, ins, scratch=(), mib=8, us=2):
    specs = [SMEM if space == "s" else VMEM for space, _ in ins]
    return pl.pallas_call(
        kernel,
        name=name,
        out_shape=outs,
        in_specs=specs,
        out_specs=tuple(VMEM for _ in outs),
        scratch_shapes=list(scratch),
        compiler_params=pltpu.CompilerParams(vmem_limit_bytes=mib << 20),
        cost_estimate=pl.CostEstimate(flops=us * 10**9, bytes_accessed=us * 10**6, transcendentals=0),
    )(*[array for _, array in ins])


def split3(x):
    first = x.astype(BF).astype(F)
    rest = x - first
    second = rest.astype(BF).astype(F)
    return first, second, (rest - second).astype(BF).astype(F)


def slot_table(listed):
    listed = listed.astype(F).T.astype(I)
    owner = listed >> 6
    local = (listed & 63) + 1
    lanes = lax.broadcasted_iota(I, (BOX_DEV, DEVICES), 1)
    table = jnp.zeros((BOX_DEV, DEVICES), I)
    for k in range(listed.shape[1]):
        hit = owner[:, k : k + 1] == lanes
        table = jnp.where(hit, local[:, k : k + 1], table)
    table = table.astype(F)
    used = table > 0.0
    row = lax.broadcasted_iota(I, (BOX_DEV, BOX_DEV), 0)
    col = lax.broadcasted_iota(I, (BOX_DEV, BOX_DEV), 1)
    before = (col < row).astype(F).astype(BF)
    rank = jnp.dot(before, used.astype(F).astype(BF), preferred_element_type=F)
    return table, jnp.where(used, rank, -1.0)


def prep_kernel(list_ref, node_ref, o_ref):
    table, slot = slot_table(list_ref[...])
    slot_t = slot.T
    nodes = jnp.concatenate([node_ref[c] for c in range(3)], 1)
    parts = [p.astype(BF) for p in split3(nodes)]
    ids = []
    for j in range(SLOTS):
        at = float(j)
        ids.append(jnp.sum(jnp.where(slot == at, table - 1.0, 0.0), axis=0, keepdims=True))
        sel = (slot_t == at).astype(F).astype(BF)
        got = sum(jnp.dot(sel, p, preferred_element_type=F) for p in parts)
        for c in range(3):
            o_ref[pl.ds(c * SLOTS + j, DEVICES, stride=ASK), :] = got[:, c * 128 : (c + 1) * 128]
    stacked = jnp.concatenate(ids + [jnp.zeros((128 - SLOTS, 128), F)], 0).T
    o_ref[pl.ds(ASK - 1, DEVICES, stride=ASK), :] = stacked


def feat_kernel(cen_ref, coef_ref, rad_ref, a_ref, cf_ref):
    def one(g, carry):
        c = cen_ref[:, pl.ds(g, 1), :].reshape(3, 128)
        r = rad_ref[pl.ds(g, 1), :]
        inv = 1.0 / (r * r)
        sq = c[0:1] * c[0:1] + c[1:2] * c[1:2] + c[2:3] * c[2:3]
        f = jnp.concatenate([c * (-2.0 * inv), inv, inv * sq, jnp.zeros((3, 128), F)], 0)
        p, q, t = split3(f)
        s = jnp.concatenate([p, p, p, q, q, t, jnp.zeros((80, 128), F)], 0)
        a_ref[pl.ds(pl.multiple_of(g * 128, 128), 128), :] = s.T.astype(BF)
        ks = split3(4.0 * coef_ref[:, pl.ds(g, 1), :].reshape(3, 128))
        z = jnp.concatenate([*ks, jnp.zeros((7, 128), F)], 0).astype(BF)
        cf_ref[pl.ds(pl.multiple_of(g * 16, 16), 16), :] = jnp.concatenate([z, z], 1)
        return carry

    lax.fori_loop(0, 64, one, 0)


def terms_kernel(x_ref, a_ref, cf_ref, o_ref, v_ref, b_ref, q_ref, w_ref, stage_ref, ids_ref, sem):
    stage_ref[...] = x_ref[pl.ds(ASK - 1, DEVICES, stride=ASK), :].T[0:SLOTS].astype(I)
    copy = pltpu.make_async_copy(stage_ref, ids_ref, sem)
    copy.start()
    for buf in range(2):
        for j in range(SLOTS):
            b_ref[buf, j, 48:128, :] = jnp.zeros((80, 128), BF)
        for k in range(3):
            v_ref[buf, k, pl.ds(32, 32), :] = jnp.zeros((32, 128), F)
        v_ref[buf, 0, pl.ds(32, 8), :] = jnp.ones((8, 128), F)
    copy.wait()

    def stage0(i, buf):
        base = jnp.minimum(i, DEVICES - 1) * ASK
        x, y, z = [x_ref[pl.ds(base + c * SLOTS, SLOTS), :] for c in range(3)]
        for f, value in enumerate((x, y, z, x * x + y * y + z * z)):
            first = value.astype(BF).astype(F)
            rest = value - first
            second = rest.astype(BF).astype(F)
            for k, part in enumerate((first, second, rest - second)):
                v_ref[buf, k, pl.ds(f * 8, 8), :] = part
        for j in range(SLOTS):
            v = [v_ref[buf, k, pl.ds(j, 8, stride=8), :] for k in range(3)]
            b_ref[buf, j, 0:48, :] = jnp.concatenate(
                [v[0], v[1], v[2], v[0], v[1], v[0]], 0
            ).astype(BF)

    def stage1(i, buf, j):
        g = ids_ref[j, jnp.minimum(i, DEVICES - 1)]
        a = a_ref[pl.ds(pl.multiple_of(g * 128, 128), 128), :]
        q_ref[buf, j] = jnp.dot(a, b_ref[buf, j], preferred_element_type=F)

    def stage2(buf, j):
        m = jnp.maximum(q_ref[buf, j], TINY)
        q = m * lax.rsqrt(m)
        t = jnp.maximum(1.0 - q, 0.0)
        t = t * t
        w = (t * t) * (q + 0.25)
        high = w.astype(BF)
        w_ref[buf, j, 0:128, :] = high
        w_ref[buf, j, 128:256, :] = (w - high.astype(F)).astype(BF)

    def stage3(i, buf, j):
        base = pl.multiple_of(i * GIVE, GIVE)
        g = ids_ref[j, i]
        c = cf_ref[pl.ds(pl.multiple_of(g * 16, 16), 16), :]
        r = jnp.dot(c, w_ref[buf, j], preferred_element_type=F)
        o_ref[pl.ds(base + j, 3, stride=SLOTS), :] = r[0:3] + r[3:6] + r[6:9]

    slots = range(SLOTS)
    stage0(0, 0)
    stage0(1, 1)
    for j in slots:
        stage1(0, 0, j)
    stage0(2, 0)
    for j in slots:
        stage1(1, 1, j)
    for j in slots:
        stage2(0, j)

    def some(h, carry):
        for u in range(UNROLL):
            i = h * UNROLL + u
            buf = u % 2
            for j in slots:
                stage1(i + 2, buf, j)
                stage2(1 - buf, j)
                stage3(i, buf, j)
            stage0(i + 3, 1 - buf)
        return carry

    lax.fori_loop(0, DEVICES // UNROLL, some, 0)


def sum_kernel(list_ref, back_ref, o_ref):
    _, slot = slot_table(list_ref[...])
    acc = jnp.zeros((BOX_DEV, 384), F)
    for j in range(SLOTS):
        sel = (slot == float(j)).astype(F).astype(BF)
        terms = jnp.concatenate(
            [back_ref[pl.ds(c * SLOTS + j, DEVICES, stride=GIVE), :] for c in range(3)], 1
        )
        for part in split3(terms):
            acc = acc + jnp.dot(sel, part.astype(BF), preferred_element_type=F)
    for c in range(3):
        o_ref[c * BOX_DEV : (c + 1) * BOX_DEV, :] = acc[:, c * 128 : (c + 1) * 128]


def reduce_kernel(node_ref, own_ref, one_ref, two_ref, three_ref, d_ref, up_ref, down_ref):
    d_ref[...] = own_ref[...] + one_ref[...] + two_ref[...] + three_ref[...]
    zero = jnp.zeros((HALO, 128), F)
    x = [node_ref[c] for c in range(3)]
    d = [d_ref[c * BOX_DEV : (c + 1) * BOX_DEV, :] for c in range(3)]
    for ref, first in ((up_ref, BOX_DEV - HALO), (down_ref, 0)):
        ref[...] = jnp.concatenate([t[first : first + HALO] for t in x + d] + [zero, zero], 0)


def face_kernel(where_ref, near_ref, node_ref, d_ref, low_ref, high_ref, face_ref, v_ref, s_ref, tab_ref, cor_ref, code_ref):
    origin = where_ref[0] * BOX_DEV - HALO
    for c in range(6):
        own = node_ref[c] if c < 3 else d_ref[(c - 3) * BOX_DEV : (c - 2) * BOX_DEV, :]
        edge = slice(c * HALO, (c + 1) * HALO)
        tab_ref[pl.ds(c, NEAR, stride=8), :] = jnp.concatenate(
            [low_ref[edge, :], own, high_ref[edge, :]], 0
        )
    for c in (6, 7):
        tab_ref[pl.ds(c, NEAR, stride=8), :] = jnp.zeros((NEAR, 128), F)
    for k in range(3):
        for h in range(2):
            code_ref[pl.ds((k * 2 + h) * BOX_DEV, BOX_DEV), :] = face_ref[
                k, :, h * 128 : (h + 1) * 128
            ]

    def some(g, carry):
        for u in range(8):
            b = g * 8 + u
            tables = []
            for j in range(8):
                at = near_ref[j, b] - origin
                tables.append(tab_ref[pl.ds(pl.multiple_of(at * 8, 8), 8), :])
            for h in range(2):
                for k in range(3):
                    code = code_ref[pl.ds((k * 2 + h) * BOX_DEV + b, 1), :]
                    code = jnp.broadcast_to(code, (8, 128))
                    lane = code & 127
                    which = code >> 7
                    got = None
                    for j in range(8):
                        value = jnp.take_along_axis(tables[j], lane, axis=1)
                        got = value if got is None else jnp.where(which == j, value, got)
                    cor_ref[k, pl.ds(h * BOX_DEV + b, 8, stride=128), :] = got
        return carry

    lax.fori_loop(0, BOX_DEV // 8, some, 0)

    for h in range(2):

        def corner(k):
            part = [cor_ref[k, pl.ds(c * 128 + h * BOX_DEV, BOX_DEV), :] for c in range(6)]
            return [part[c] + 0.5 * part[c + 3] for c in range(3)], part[3:6]

        (ma, da), (mb, db), (mc, dc) = corner(0), corner(1), corner(2)
        u = [mb[c] - ma[c] for c in range(3)]
        w = [mc[c] - ma[c] for c in range(3)]
        swept = None
        for c in range(3):
            p, q = (c + 1) % 3, (c + 2) % 3
            normal = 0.5 * (u[p] * w[q] - u[q] * w[p])
            term = ((da[c] + db[c] + dc[c]) / 3.0) * normal
            swept = term if swept is None else swept + term
        s_ref[:, h * 128 : (h + 1) * 128] = swept
    for c in range(3):
        v_ref[c] = d_ref[c * BOX_DEV : (c + 1) * BOX_DEV, :] * 2.0


def to_all(array):
    rows = array.shape[0] // DEVICES
    packets = array.reshape(DEVICES, rows, 1, 128)
    packets = lax.all_to_all(packets, BOTH, split_axis=0, concat_axis=0, tiled=True)
    return packets.reshape(DEVICES * rows, 128)


def around(array):
    return [lax.ppermute(array, "surf", [(i, (i + k) % 4) for i in range(4)]) for k in (1, 2, 3)]


def shape(*dims, kind=F):
    return jax.ShapeDtypeStruct(dims, kind)


def body(node_pos, centres, coefs, radii, block_list, neighbours, faces):
    listed = block_list[0].T
    nodes, cens, weights = [a.transpose(1, 0, 2) for a in (node_pos, centres, coefs)]
    where = lax.axis_index("vol").astype(I).reshape(1)
    (sent,) = call(
        prep_kernel,
        "prep",
        (shape(DEVICES * ASK, 128),),
        [("v", listed), ("v", nodes)],
    )
    tables = call(
        feat_kernel,
        "feats",
        (shape(64 * 128, 128, kind=BF), shape(64 * 16, 256, kind=BF)),
        [("v", cens), ("v", weights), ("v", radii)],
        us=10,
    )
    (terms,) = call(
        terms_kernel,
        "terms",
        (shape(DEVICES * GIVE, 128),),
        [("v", to_all(sent)), ("v", tables[0]), ("v", tables[1])],
        [
            pltpu.VMEM((2, 3, 64, 128), F),
            pltpu.VMEM((2, SLOTS, 128, 128), BF),
            pltpu.VMEM((2, SLOTS, 128, 128), F),
            pltpu.VMEM((2, SLOTS, 256, 128), BF),
            pltpu.VMEM((SLOTS, 128), I),
            pltpu.SMEM((SLOTS, 128), I),
            pltpu.SemaphoreType.DMA,
        ],
        mib=16,
        us=45,
    )
    (own,) = call(
        sum_kernel,
        "sums",
        (shape(3 * BOX_DEV, 128),),
        [("v", listed), ("v", to_all(terms))],
    )
    d, up, down = call(
        reduce_kernel,
        "reduce",
        (shape(3 * BOX_DEV, 128), shape(32, 128), shape(32, 128)),
        [("v", nodes), ("v", own)] + [("v", r) for r in around(own)],
    )
    low = lax.ppermute(up, "vol", [(i, i + 1) for i in range(31)])
    high = lax.ppermute(down, "vol", [(i + 1, i) for i in range(31)])
    velocity, swept = call(
        face_kernel,
        "faces",
        (shape(3, BOX_DEV, 128), shape(BOX_DEV, 256)),
        [("s", where), ("s", neighbours.T), ("v", nodes), ("v", d), ("v", low), ("v", high)]
        + [("v", faces.transpose(1, 0, 2))],
        [
            pltpu.VMEM((8 * NEAR, 128), F),
            pltpu.VMEM((3, 1024, 128), F),
            pltpu.VMEM((6 * BOX_DEV, 128), I),
        ],
    )
    return velocity.transpose(1, 0, 2), swept


def solution(mesh):
    placed = (
        P("vol", None, None),
        P(("vol", "surf"), None, None),
        P(("vol", "surf"), None, None),
        P(("vol", "surf"), None),
        P("surf", "vol", None),
        P("vol", None),
        P("vol", None, None),
    )
    return jax.shard_map(
        body,
        mesh=mesh,
        in_specs=placed,
        out_specs=(P("vol", None, None), P("vol", None)),
        check_vma=False,
    )
```

```python
import functools

import jax
import jax.numpy as jnp
from jax import lax
from jax.experimental import pallas as pl
from jax.experimental.pallas import tpu as pltpu
from jax.sharding import PartitionSpec as P

BF = jnp.bfloat16
F = jnp.float32
I = jnp.int32
BOTH = ("vol", "surf")
DEVICES = 128
SLOTS = 8
ASK = 3 * SLOTS + 1
GIVE = 3 * SLOTS
UNROLL = 8
BOX_DEV = 64
HALO = 4
NEAR = BOX_DEV + 2 * HALO
TINY = 1e-30
VMEM = pl.BlockSpec(memory_space=pltpu.VMEM)
SMEM = pl.BlockSpec(memory_space=pltpu.SMEM)


def call(kernel, name, outs, ins, scratch=(), mib=8, us=2):
    specs = [SMEM if space == "s" else VMEM for space, _ in ins]
    return pl.pallas_call(
        kernel,
        name=name,
        out_shape=outs,
        in_specs=specs,
        out_specs=tuple(VMEM for _ in outs),
        scratch_shapes=list(scratch),
        compiler_params=pltpu.CompilerParams(vmem_limit_bytes=mib << 20),
        cost_estimate=pl.CostEstimate(flops=us * 10**9, bytes_accessed=us * 10**6, transcendentals=0),
    )(*[array for _, array in ins])


def split3(x):
    first = x.astype(BF).astype(F)
    rest = x - first
    second = rest.astype(BF).astype(F)
    return first, second, (rest - second).astype(BF).astype(F)


def slot_table(listed):
    listed = listed.astype(F).T.astype(I)
    owner = listed >> 6
    local = (listed & 63) + 1
    lanes = lax.broadcasted_iota(I, (BOX_DEV, DEVICES), 1)
    table = jnp.zeros((BOX_DEV, DEVICES), I)
    for k in range(listed.shape[1]):
        hit = owner[:, k : k + 1] == lanes
        table = jnp.where(hit, local[:, k : k + 1], table)
    table = table.astype(F)
    used = table > 0.0
    row = lax.broadcasted_iota(I, (BOX_DEV, BOX_DEV), 0)
    col = lax.broadcasted_iota(I, (BOX_DEV, BOX_DEV), 1)
    before = (col < row).astype(F).astype(BF)
    rank = jnp.dot(before, used.astype(F).astype(BF), preferred_element_type=F)
    return table, jnp.where(used, rank, -1.0)


def prep_kernel(list_ref, node_ref, o_ref):
    table, slot = slot_table(list_ref[...])
    slot_t = slot.T
    nodes = jnp.concatenate([node_ref[c] for c in range(3)], 1)
    parts = [p.astype(BF) for p in split3(nodes)]
    ids = []
    for j in range(SLOTS):
        at = float(j)
        ids.append(jnp.sum(jnp.where(slot == at, table - 1.0, 0.0), axis=0, keepdims=True))
        sel = (slot_t == at).astype(F).astype(BF)
        got = sum(jnp.dot(sel, p, preferred_element_type=F) for p in parts)
        for c in range(3):
            o_ref[pl.ds(c * SLOTS + j, DEVICES, stride=ASK), :] = got[:, c * 128 : (c + 1) * 128]
    stacked = jnp.concatenate(ids + [jnp.zeros((128 - SLOTS, 128), F)], 0).T
    o_ref[pl.ds(ASK - 1, DEVICES, stride=ASK), :] = stacked


def feat_kernel(cen_ref, coef_ref, rad_ref, a_ref, cf_ref):
    def one(g, carry):
        c = cen_ref[:, pl.ds(g, 1), :].reshape(3, 128)
        r = rad_ref[pl.ds(g, 1), :]
        inv = 1.0 / (r * r)
        sq = c[0:1] * c[0:1] + c[1:2] * c[1:2] + c[2:3] * c[2:3]
        f = jnp.concatenate([c * (-2.0 * inv), inv, inv * sq, jnp.zeros((3, 128), F)], 0)
        p, q, t = split3(f)
        s = jnp.concatenate([p, p, p, q, q, t, jnp.zeros((80, 128), F)], 0)
        a_ref[pl.ds(pl.multiple_of(g * 128, 128), 128), :] = s.T.astype(BF)
        ks = split3(4.0 * coef_ref[:, pl.ds(g, 1), :].reshape(3, 128))
        z = jnp.concatenate([ks[0], ks[1], jnp.zeros((10, 128), F)], 0).astype(BF)
        cf_ref[pl.ds(pl.multiple_of(g * 16, 16), 16), :] = jnp.concatenate([z, z], 1)
        return carry

    lax.fori_loop(0, 64, one, 0)


def terms_kernel(
    x_ref, a_ref, cf_ref, o_ref, v_ref, b_ref, q_ref, w_ref, r_ref, stage_ref, ids_ref, sem
):
    stage_ref[...] = x_ref[pl.ds(ASK - 1, DEVICES, stride=ASK), :].T[0:SLOTS].astype(I)
    copy = pltpu.make_async_copy(stage_ref, ids_ref, sem)
    copy.start()
    for buf in range(2):
        for j in range(SLOTS):
            b_ref[buf, j, 48:128, :] = jnp.zeros((80, 128), BF)
        for k in range(3):
            v_ref[buf, k, pl.ds(32, 32), :] = jnp.zeros((32, 128), F)
        v_ref[buf, 0, pl.ds(32, 8), :] = jnp.ones((8, 128), F)
    copy.wait()

    def stage0(i, buf):
        i = jnp.minimum(i, DEVICES - 1)
        base = i * ASK
        x, y, z = [x_ref[pl.ds(base + c * SLOTS, SLOTS), :] for c in range(3)]
        for f, value in enumerate((x, y, z, x * x + y * y + z * z)):
            first = value.astype(BF).astype(F)
            rest = value - first
            second = rest.astype(BF).astype(F)
            for k, part in enumerate((first, second, rest - second)):
                v_ref[buf, k, pl.ds(f * 8, 8), :] = part
        for j in range(SLOTS):
            v = [v_ref[buf, k, pl.ds(j, 8, stride=8), :] for k in range(3)]
            b_ref[buf, j, 0:48, :] = jnp.concatenate(
                [v[0], v[1], v[2], v[0], v[1], v[0]], 0
            ).astype(BF)

    def stage1(i, buf, j):
        g = ids_ref[j, jnp.minimum(i, DEVICES - 1)]
        a = a_ref[pl.ds(pl.multiple_of(g * 128, 128), 128), :]
        q_ref[buf, j] = jnp.dot(a, b_ref[buf, j], preferred_element_type=F)

    def stage2(buf, j):
        m = jnp.maximum(q_ref[buf, j], TINY)
        q = m * lax.rsqrt(m)
        t = jnp.maximum(1.0 - q, 0.0)
        t = t * t
        w = (t * t) * (q + 0.25)
        high = w.astype(BF)
        w_ref[buf, j, 0:128, :] = high
        w_ref[buf, j, 128:256, :] = (w - high.astype(F)).astype(BF)

    def stage3(i, buf, j):
        g = ids_ref[j, i]
        c = cf_ref[pl.ds(pl.multiple_of(g * 16, 16), 16), :]
        r = jnp.dot(c, w_ref[buf, j], preferred_element_type=F)
        r_ref[buf, pl.ds(j, 6, stride=SLOTS), :] = r[0:6]

    def stage4(i, buf):
        base = pl.multiple_of(i * GIVE, GIVE)
        o_ref[pl.ds(base, GIVE), :] = r_ref[buf, 0:GIVE, :] + r_ref[buf, GIVE : 2 * GIVE, :]

    slots = range(SLOTS)
    stage0(0, 0)
    stage0(1, 1)
    for j in slots:
        stage1(0, 0, j)
    stage0(2, 0)
    for j in slots:
        stage1(1, 1, j)
    for j in slots:
        stage2(0, j)

    def some(h, carry):
        for u in range(UNROLL):
            i = h * UNROLL + u
            buf = u % 2
            for j in slots:
                stage1(i + 2, buf, j)
                stage2(1 - buf, j)
                stage3(i, buf, j)
            stage4(i, buf)
            stage0(i + 3, 1 - buf)
        return carry

    lax.fori_loop(0, DEVICES // UNROLL, some, 0)


def sum_kernel(list_ref, back_ref, o_ref):
    _, slot = slot_table(list_ref[...])
    acc = jnp.zeros((BOX_DEV, 384), F)
    for j in range(SLOTS):
        sel = (slot == float(j)).astype(F).astype(BF)
        terms = jnp.concatenate(
            [back_ref[pl.ds(c * SLOTS + j, DEVICES, stride=GIVE), :] for c in range(3)], 1
        )
        for part in split3(terms):
            acc = acc + jnp.dot(sel, part.astype(BF), preferred_element_type=F)
    for c in range(3):
        o_ref[c * BOX_DEV : (c + 1) * BOX_DEV, :] = acc[:, c * 128 : (c + 1) * 128]


def reduce_kernel(node_ref, own_ref, one_ref, two_ref, three_ref, d_ref, up_ref, down_ref):
    d_ref[...] = own_ref[...] + one_ref[...] + two_ref[...] + three_ref[...]
    zero = jnp.zeros((HALO, 128), F)
    x = [node_ref[c] for c in range(3)]
    d = [d_ref[c * BOX_DEV : (c + 1) * BOX_DEV, :] for c in range(3)]
    for ref, first in ((up_ref, BOX_DEV - HALO), (down_ref, 0)):
        ref[...] = jnp.concatenate([t[first : first + HALO] for t in x + d] + [zero, zero], 0)


def corners(near_ref, tab_ref, code_ref, cor_ref, box, at, origin, count):
    tables = []
    for j in range(8):
        row = near_ref[j, box] - origin
        tables.append(tab_ref[pl.ds(pl.multiple_of(row * 8, 8), 8), :])
    for h in range(2):
        for k in range(3):
            code = code_ref[pl.ds((k * 2 + h) * BOX_DEV + box, 1), :]
            code = jnp.broadcast_to(code, (8, 128))
            lane = code & 127
            which = code >> 7
            got = None
            for j in range(8):
                value = jnp.take_along_axis(tables[j], lane, axis=1)
                got = value if got is None else jnp.where(which == j, value, got)
            cor_ref[k, pl.ds(h * count + at, 8, stride=2 * count), :] = got


def volumes(cor_ref, h, count):
    def corner(k):
        part = [cor_ref[k, pl.ds((c * 2 + h) * count, count), :] for c in range(6)]
        return [part[c] + 0.5 * part[c + 3] for c in range(3)], part[3:6]

    (ma, da), (mb, db), (mc, dc) = corner(0), corner(1), corner(2)
    u = [mb[c] - ma[c] for c in range(3)]
    w = [mc[c] - ma[c] for c in range(3)]
    swept = None
    for c in range(3):
        p, q = (c + 1) % 3, (c + 2) % 3
        normal = 0.5 * (u[p] * w[q] - u[q] * w[p])
        term = ((da[c] + db[c] + dc[c]) / 3.0) * normal
        swept = term if swept is None else swept + term
    return swept


def split_codes(face_ref, code_ref):
    for k in range(3):
        for h in range(2):
            code_ref[pl.ds((k * 2 + h) * BOX_DEV, BOX_DEV), :] = face_ref[
                k, :, h * 128 : (h + 1) * 128
            ]


def inner_kernel(where_ref, near_ref, node_ref, d_ref, face_ref, v_ref, s_ref, tab_ref, cor_ref, code_ref):
    for c in range(6):
        own = node_ref[c] if c < 3 else d_ref[(c - 3) * BOX_DEV : (c - 2) * BOX_DEV, :]
        tab_ref[pl.ds(c, BOX_DEV, stride=8), :] = own
    for c in (6, 7):
        tab_ref[pl.ds(c, BOX_DEV, stride=8), :] = jnp.zeros((BOX_DEV, 128), F)
    split_codes(face_ref, code_ref)
    origin = where_ref[0] * BOX_DEV

    def some(g, carry):
        for u in range(8):
            box = g * 8 + HALO + u
            corners(near_ref, tab_ref, code_ref, cor_ref, box, box, origin, BOX_DEV)
        return carry

    lax.fori_loop(0, (BOX_DEV - 2 * HALO) // 8, some, 0)
    for h in range(2):
        s_ref[:, h * 128 : (h + 1) * 128] = volumes(cor_ref, h, BOX_DEV)
    for c in range(3):
        v_ref[c] = d_ref[c * BOX_DEV : (c + 1) * BOX_DEV, :] * 2.0


def edge_kernel(
    where_ref, near_ref, node_ref, d_ref, low_ref, high_ref, face_ref, in_ref, s_ref, tab_ref, cor_ref, code_ref
):
    for c in range(6):
        own = node_ref[c] if c < 3 else d_ref[(c - 3) * BOX_DEV : (c - 2) * BOX_DEV, :]
        edge = slice(c * HALO, (c + 1) * HALO)
        tab_ref[pl.ds(c, NEAR, stride=8), :] = jnp.concatenate(
            [low_ref[edge, :], own, high_ref[edge, :]], 0
        )
    for c in (6, 7):
        tab_ref[pl.ds(c, NEAR, stride=8), :] = jnp.zeros((NEAR, 128), F)
    split_codes(face_ref, code_ref)
    origin = where_ref[0] * BOX_DEV - HALO
    for at in range(2 * HALO):
        box = at if at < HALO else BOX_DEV - 2 * HALO + at
        corners(near_ref, tab_ref, code_ref, cor_ref, box, at, origin, 2 * HALO)
    s_ref[...] = in_ref[...]
    for h in range(2):
        swept = volumes(cor_ref, h, 2 * HALO)
        s_ref[0:HALO, h * 128 : (h + 1) * 128] = swept[0:HALO]
        s_ref[BOX_DEV - HALO : BOX_DEV, h * 128 : (h + 1) * 128] = swept[HALO:]


def to_all(array):
    rows = array.shape[0] // DEVICES
    packets = array.reshape(DEVICES, rows, 1, 128)
    packets = lax.all_to_all(packets, BOTH, split_axis=0, concat_axis=0, tiled=True)
    return packets.reshape(DEVICES * rows, 128)


def around(array):
    return [lax.ppermute(array, "surf", [(i, (i + k) % 4) for i in range(4)]) for k in (1, 2, 3)]


def shape(*dims, kind=F):
    return jax.ShapeDtypeStruct(dims, kind)


def body(node_pos, centres, coefs, radii, block_list, neighbours, faces):
    listed = block_list[0].T
    nodes, cens, weights = [a.transpose(1, 0, 2) for a in (node_pos, centres, coefs)]
    where = lax.axis_index("vol").astype(I).reshape(1)
    (sent,) = call(
        prep_kernel,
        "prep",
        (shape(DEVICES * ASK, 128),),
        [("v", listed), ("v", nodes)],
    )
    tables = call(
        feat_kernel,
        "feats",
        (shape(64 * 128, 128, kind=BF), shape(64 * 16, 256, kind=BF)),
        [("v", cens), ("v", weights), ("v", radii)],
        us=10,
    )
    (terms,) = call(
        terms_kernel,
        "terms",
        (shape(DEVICES * GIVE, 128),),
        [("v", to_all(sent)), ("v", tables[0]), ("v", tables[1])],
        [
            pltpu.VMEM((2, 3, 64, 128), F),
            pltpu.VMEM((2, SLOTS, 128, 128), BF),
            pltpu.VMEM((2, SLOTS, 128, 128), F),
            pltpu.VMEM((2, SLOTS, 256, 128), BF),
            pltpu.VMEM((2, 2 * GIVE, 128), F),
            pltpu.VMEM((SLOTS, 128), I),
            pltpu.SMEM((SLOTS, 128), I),
            pltpu.SemaphoreType.DMA,
        ],
        mib=16,
        us=45,
    )
    (own,) = call(
        sum_kernel,
        "sums",
        (shape(3 * BOX_DEV, 128),),
        [("v", listed), ("v", to_all(terms))],
    )
    d, up, down = call(
        reduce_kernel,
        "reduce",
        (shape(3 * BOX_DEV, 128), shape(32, 128), shape(32, 128)),
        [("v", nodes), ("v", own)] + [("v", r) for r in around(own)],
    )
    low = lax.ppermute(up, "vol", [(i, i + 1) for i in range(31)])
    high = lax.ppermute(down, "vol", [(i + 1, i) for i in range(31)])
    near, codes = neighbours.T, faces.transpose(1, 0, 2)
    velocity, inner = call(
        inner_kernel,
        "inner",
        (shape(3, BOX_DEV, 128), shape(BOX_DEV, 256)),
        [("s", where), ("s", near), ("v", nodes), ("v", d), ("v", codes)],
        [
            pltpu.VMEM((8 * BOX_DEV, 128), F),
            pltpu.VMEM((3, 16 * BOX_DEV, 128), F),
            pltpu.VMEM((6 * BOX_DEV, 128), I),
        ],
        us=6,
    )
    (swept,) = call(
        edge_kernel,
        "edges",
        (shape(BOX_DEV, 256),),
        [("s", where), ("s", near), ("v", nodes), ("v", d), ("v", low), ("v", high), ("v", codes), ("v", inner)],
        [
            pltpu.VMEM((8 * NEAR, 128), F),
            pltpu.VMEM((3, 128, 128), F),
            pltpu.VMEM((6 * BOX_DEV, 128), I),
        ],
    )
    return velocity.transpose(1, 0, 2), swept


def solution(mesh):
    placed = (
        P("vol", None, None),
        P(("vol", "surf"), None, None),
        P(("vol", "surf"), None, None),
        P(("vol", "surf"), None),
        P("surf", "vol", None),
        P("vol", None),
        P("vol", None, None),
    )
    return jax.shard_map(
        body,
        mesh=mesh,
        in_specs=placed,
        out_specs=(P("vol", None, None), P("vol", None)),
        check_vma=False,
    )
```

```python
import functools

import jax
import jax.numpy as jnp
from jax import lax
from jax.experimental import pallas as pl
from jax.experimental.pallas import tpu as pltpu
from jax.sharding import PartitionSpec as P

BF = jnp.bfloat16
F = jnp.float32
I = jnp.int32
BOTH = ("vol", "surf")
DEVICES = 128
SLOTS = 8
ASK = 3 * SLOTS + 1
GIVE = 3 * SLOTS
UNROLL = 8
BOX_DEV = 64
HALO = 4
NEAR = BOX_DEV + 2 * HALO
TINY = 1e-30
VMEM = pl.BlockSpec(memory_space=pltpu.VMEM)
SMEM = pl.BlockSpec(memory_space=pltpu.SMEM)


def call(kernel, name, outs, ins, scratch=(), mib=8, us=2):
    specs = [SMEM if space == "s" else VMEM for space, _ in ins]
    return pl.pallas_call(
        kernel,
        name=name,
        out_shape=outs,
        in_specs=specs,
        out_specs=tuple(VMEM for _ in outs),
        scratch_shapes=list(scratch),
        compiler_params=pltpu.CompilerParams(vmem_limit_bytes=mib << 20),
        cost_estimate=pl.CostEstimate(flops=us * 10**9, bytes_accessed=us * 10**6, transcendentals=0),
    )(*[array for _, array in ins])


def split3(x):
    first = x.astype(BF).astype(F)
    rest = x - first
    second = rest.astype(BF).astype(F)
    return first, second, (rest - second).astype(BF).astype(F)


def slot_table(listed):
    listed = listed.astype(F).T.astype(I)
    owner = listed >> 6
    local = (listed & 63) + 1
    lanes = lax.broadcasted_iota(I, (BOX_DEV, DEVICES), 1)
    table = jnp.zeros((BOX_DEV, DEVICES), I)
    for k in range(listed.shape[1]):
        hit = owner[:, k : k + 1] == lanes
        table = jnp.where(hit, local[:, k : k + 1], table)
    table = table.astype(F)
    used = table > 0.0
    row = lax.broadcasted_iota(I, (BOX_DEV, BOX_DEV), 0)
    col = lax.broadcasted_iota(I, (BOX_DEV, BOX_DEV), 1)
    before = (col < row).astype(F).astype(BF)
    rank = jnp.dot(before, used.astype(F).astype(BF), preferred_element_type=F)
    return table, jnp.where(used, rank, -1.0)


def prep_kernel(list_ref, node_ref, o_ref):
    table, slot = slot_table(list_ref[...])
    slot_t = slot.T
    nodes = jnp.concatenate([node_ref[c] for c in range(3)], 1)
    parts = [p.astype(BF) for p in split3(nodes)]
    ids = []
    for j in range(SLOTS):
        at = float(j)
        ids.append(jnp.sum(jnp.where(slot == at, table - 1.0, 0.0), axis=0, keepdims=True))
        sel = (slot_t == at).astype(F).astype(BF)
        got = sum(jnp.dot(sel, p, preferred_element_type=F) for p in parts)
        for c in range(3):
            o_ref[pl.ds(c * SLOTS + j, DEVICES, stride=ASK), :] = got[:, c * 128 : (c + 1) * 128]
    stacked = jnp.concatenate(ids + [jnp.zeros((128 - SLOTS, 128), F)], 0).T
    o_ref[pl.ds(ASK - 1, DEVICES, stride=ASK), :] = stacked


def feat_kernel(where_ref, own_ref, one_ref, two_ref, three_ref, a_ref, cf_ref):
    for k, ref in enumerate((own_ref, one_ref, two_ref, three_ref)):
        first = ((where_ref[1] + 4 - k) & 3) * BOX_DEV

        def some(h, carry):
            base = pl.multiple_of(h * 8, 8)
            x, y, z, r, kx, ky, kz = [ref[pl.ds(c * BOX_DEV + base, 8), :] for c in range(7)]
            inv = 1.0 / (r * r)
            scale = -2.0 * inv
            rows = [x * scale, y * scale, z * scale, inv, inv * (x * x + y * y + z * z)]
            rows = [split3(t) for t in rows]
            ks = [split3(4.0 * t) for t in (kx, ky, kz)]
            for u in range(8):
                def part(n):
                    return [t[n][u : u + 1] for t in rows] + [jnp.zeros((3, 128), F)]

                p, q, t = part(0), part(1), part(2)
                s = jnp.concatenate(p * 3 + q * 2 + t, 0).astype(BF)
                at = first + base + u
                a_ref[pl.ds(pl.multiple_of(at * 48, 16), 48), :] = s
                c = jnp.concatenate(
                    [t[n][u : u + 1] for n in range(2) for t in ks] + [jnp.zeros((10, 128), F)], 0
                ).astype(BF)
                cf_ref[pl.ds(pl.multiple_of(at * 16, 16), 16), :] = c
            return carry

        lax.fori_loop(0, BOX_DEV // 8, some, 0)


def terms_kernel(
    x_ref, a_ref, cf_ref, o_ref, v_ref, b_ref, q_ref, w_ref, r_ref, stage_ref, ids_ref, sem
):
    stage_ref[...] = x_ref[pl.ds(ASK - 1, DEVICES, stride=ASK), :].T[0:SLOTS].astype(I)
    copy = pltpu.make_async_copy(stage_ref, ids_ref, sem)
    copy.start()
    for buf in range(2):
        for k in range(3):
            v_ref[buf, k, pl.ds(32, 32), :] = jnp.zeros((32, 128), F)
        v_ref[buf, 0, pl.ds(32, 8), :] = jnp.ones((8, 128), F)
    copy.wait()

    def stage0(i, buf):
        i = jnp.minimum(i, DEVICES - 1)
        base = i * ASK
        x, y, z = [x_ref[pl.ds(base + c * SLOTS, SLOTS), :] for c in range(3)]
        for f, value in enumerate((x, y, z, x * x + y * y + z * z)):
            first = value.astype(BF).astype(F)
            rest = value - first
            second = rest.astype(BF).astype(F)
            for k, part in enumerate((first, second, rest - second)):
                v_ref[buf, k, pl.ds(f * 8, 8), :] = part
        for j in range(SLOTS):
            v = [v_ref[buf, k, pl.ds(j, 8, stride=8), :] for k in range(3)]
            b_ref[buf, j] = jnp.concatenate(
                [v[0], v[1], v[2], v[0], v[1], v[0]], 0
            ).astype(BF)

    def stage1(i, buf, j):
        i = jnp.minimum(i, DEVICES - 1)
        g = (i & 3) * BOX_DEV + ids_ref[j, i]
        a = a_ref[pl.ds(pl.multiple_of(g * 48, 16), 48), :]
        q_ref[buf, j] = lax.dot_general(
            a, b_ref[buf, j], (((0,), (0,)), ((), ())), preferred_element_type=F
        )

    def stage2(buf, j):
        m = jnp.maximum(q_ref[buf, j], TINY)
        q = m * lax.rsqrt(m)
        t = jnp.maximum(1.0 - q, 0.0)
        t = t * t
        w = (t * t) * (q + 0.25)
        high = w.astype(BF)
        w_ref[buf, j, 0:128, :] = high
        w_ref[buf, j, 128:256, :] = (w - high.astype(F)).astype(BF)

    def stage3(i, buf, j):
        g = (i & 3) * BOX_DEV + ids_ref[j, i]
        c = cf_ref[pl.ds(pl.multiple_of(g * 16, 16), 16), :]
        c = jnp.concatenate([c, c], 1)
        r = jnp.dot(c, w_ref[buf, j], preferred_element_type=F)
        r_ref[buf, pl.ds(j, 6, stride=SLOTS), :] = r[0:6]

    def stage4(i, buf):
        base = pl.multiple_of(i * GIVE, GIVE)
        o_ref[pl.ds(base, GIVE), :] = r_ref[buf, 0:GIVE, :] + r_ref[buf, GIVE : 2 * GIVE, :]

    slots = range(SLOTS)
    stage0(0, 0)
    stage0(1, 1)
    for j in slots:
        stage1(0, 0, j)
    stage0(2, 0)
    for j in slots:
        stage1(1, 1, j)
    for j in slots:
        stage2(0, j)

    def some(h, carry):
        for u in range(UNROLL):
            i = h * UNROLL + u
            buf = u % 2
            for j in slots:
                stage1(i + 2, buf, j)
                stage2(1 - buf, j)
                stage3(i, buf, j)
            stage4(i, buf)
            stage0(i + 3, 1 - buf)
        return carry

    lax.fori_loop(0, DEVICES // UNROLL, some, 0)


def sum_kernel(list_ref, back_ref, o_ref):
    _, slot = slot_table(list_ref[...])
    acc = jnp.zeros((BOX_DEV, 384), F)
    for j in range(SLOTS):
        sel = (slot == float(j)).astype(F).astype(BF)
        terms = jnp.concatenate(
            [back_ref[pl.ds(c * SLOTS + j, DEVICES, stride=GIVE), :] for c in range(3)], 1
        )
        for part in split3(terms):
            acc = acc + jnp.dot(sel, part.astype(BF), preferred_element_type=F)
    for c in range(3):
        o_ref[c * BOX_DEV : (c + 1) * BOX_DEV, :] = acc[:, c * 128 : (c + 1) * 128]


def reduce_kernel(node_ref, own_ref, one_ref, two_ref, three_ref, d_ref, up_ref, down_ref):
    d_ref[...] = own_ref[...] + one_ref[...] + two_ref[...] + three_ref[...]
    zero = jnp.zeros((HALO, 128), F)
    x = [node_ref[c] for c in range(3)]
    d = [d_ref[c * BOX_DEV : (c + 1) * BOX_DEV, :] for c in range(3)]
    for ref, first in ((up_ref, BOX_DEV - HALO), (down_ref, 0)):
        ref[...] = jnp.concatenate([t[first : first + HALO] for t in x + d] + [zero, zero], 0)


def corners(near_ref, tab_ref, code_ref, cor_ref, box, at, origin, count):
    tables = []
    for j in range(8):
        row = near_ref[j, box] - origin
        tables.append(tab_ref[pl.ds(pl.multiple_of(row * 8, 8), 8), :])
    for h in range(2):
        for k in range(3):
            code = code_ref[pl.ds((k * 2 + h) * BOX_DEV + box, 1), :]
            code = jnp.broadcast_to(code, (8, 128))
            lane = code & 127
            which = code >> 7
            got = None
            for j in range(8):
                value = jnp.take_along_axis(tables[j], lane, axis=1)
                got = value if got is None else jnp.where(which == j, value, got)
            cor_ref[k, pl.ds(h * count + at, 8, stride=2 * count), :] = got


def volumes(cor_ref, h, count):
    def corner(k):
        part = [cor_ref[k, pl.ds((c * 2 + h) * count, count), :] for c in range(6)]
        return [part[c] + 0.5 * part[c + 3] for c in range(3)], part[3:6]

    (ma, da), (mb, db), (mc, dc) = corner(0), corner(1), corner(2)
    u = [mb[c] - ma[c] for c in range(3)]
    w = [mc[c] - ma[c] for c in range(3)]
    swept = None
    for c in range(3):
        p, q = (c + 1) % 3, (c + 2) % 3
        normal = 0.5 * (u[p] * w[q] - u[q] * w[p])
        term = ((da[c] + db[c] + dc[c]) / 3.0) * normal
        swept = term if swept is None else swept + term
    return swept


def split_codes(face_ref, code_ref):
    for k in range(3):
        for h in range(2):
            code_ref[pl.ds((k * 2 + h) * BOX_DEV, BOX_DEV), :] = face_ref[
                k, :, h * 128 : (h + 1) * 128
            ]


def inner_kernel(where_ref, near_ref, node_ref, d_ref, face_ref, v_ref, s_ref, tab_ref, cor_ref, code_ref):
    for c in range(6):
        own = node_ref[c] if c < 3 else d_ref[(c - 3) * BOX_DEV : (c - 2) * BOX_DEV, :]
        tab_ref[pl.ds(c, BOX_DEV, stride=8), :] = own
    for c in (6, 7):
        tab_ref[pl.ds(c, BOX_DEV, stride=8), :] = jnp.zeros((BOX_DEV, 128), F)
    split_codes(face_ref, code_ref)
    origin = where_ref[0] * BOX_DEV

    def some(g, carry):
        for u in range(8):
            box = g * 8 + HALO + u
            corners(near_ref, tab_ref, code_ref, cor_ref, box, box, origin, BOX_DEV)
        return carry

    lax.fori_loop(0, (BOX_DEV - 2 * HALO) // 8, some, 0)
    for h in range(2):
        s_ref[:, h * 128 : (h + 1) * 128] = volumes(cor_ref, h, BOX_DEV)
    for c in range(3):
        v_ref[c] = d_ref[c * BOX_DEV : (c + 1) * BOX_DEV, :] * 2.0


def edge_kernel(
    where_ref, near_ref, node_ref, d_ref, low_ref, high_ref, face_ref, in_ref, s_ref, tab_ref, cor_ref, code_ref
):
    for c in range(6):
        own = node_ref[c] if c < 3 else d_ref[(c - 3) * BOX_DEV : (c - 2) * BOX_DEV, :]
        edge = slice(c * HALO, (c + 1) * HALO)
        tab_ref[pl.ds(c, NEAR, stride=8), :] = jnp.concatenate(
            [low_ref[edge, :], own, high_ref[edge, :]], 0
        )
    for c in (6, 7):
        tab_ref[pl.ds(c, NEAR, stride=8), :] = jnp.zeros((NEAR, 128), F)
    split_codes(face_ref, code_ref)
    origin = where_ref[0] * BOX_DEV - HALO
    for at in range(2 * HALO):
        box = at if at < HALO else BOX_DEV - 2 * HALO + at
        corners(near_ref, tab_ref, code_ref, cor_ref, box, at, origin, 2 * HALO)
    s_ref[...] = in_ref[...]
    for h in range(2):
        swept = volumes(cor_ref, h, 2 * HALO)
        s_ref[0:HALO, h * 128 : (h + 1) * 128] = swept[0:HALO]
        s_ref[BOX_DEV - HALO : BOX_DEV, h * 128 : (h + 1) * 128] = swept[HALO:]


def to_all(array):
    peers = DEVICES // 4
    rows = array.shape[0] // peers
    packets = array.reshape(peers, rows, 1, 128)
    packets = lax.all_to_all(packets, "vol", split_axis=0, concat_axis=0, tiled=True)
    return packets.reshape(peers * rows, 128)


def around(array):
    return [lax.ppermute(array, "surf", [(i, (i + k) % 4) for i in range(4)]) for k in (1, 2, 3)]


def shape(*dims, kind=F):
    return jax.ShapeDtypeStruct(dims, kind)


def body(node_pos, centres, coefs, radii, block_list, neighbours, faces):
    listed = block_list[0].T
    nodes, cens, weights = [a.transpose(1, 0, 2) for a in (node_pos, centres, coefs)]
    where = jnp.stack([lax.axis_index("vol"), lax.axis_index("surf")]).astype(I)
    blocks = jnp.concatenate(
        [cens.reshape(3 * BOX_DEV, 128), radii, weights.reshape(3 * BOX_DEV, 128)], 0
    )
    (sent,) = call(
        prep_kernel,
        "prep",
        (shape(DEVICES * ASK, 128),),
        [("v", listed), ("v", nodes)],
    )
    tables = call(
        feat_kernel,
        "feats",
        (shape(4 * BOX_DEV * 48, 128, kind=BF), shape(4 * BOX_DEV * 16, 128, kind=BF)),
        [("s", where), ("v", blocks)] + [("v", r) for r in around(blocks)],
        us=5,
    )
    (terms,) = call(
        terms_kernel,
        "terms",
        (shape(DEVICES * GIVE, 128),),
        [("v", to_all(sent)), ("v", tables[0]), ("v", tables[1])],
        [
            pltpu.VMEM((2, 3, 64, 128), F),
            pltpu.VMEM((2, SLOTS, 48, 128), BF),
            pltpu.VMEM((2, SLOTS, 128, 128), F),
            pltpu.VMEM((2, SLOTS, 256, 128), BF),
            pltpu.VMEM((2, 2 * GIVE, 128), F),
            pltpu.VMEM((SLOTS, 128), I),
            pltpu.SMEM((SLOTS, 128), I),
            pltpu.SemaphoreType.DMA,
        ],
        mib=16,
        us=45,
    )
    (own,) = call(
        sum_kernel,
        "sums",
        (shape(3 * BOX_DEV, 128),),
        [("v", listed), ("v", to_all(terms))],
    )
    d, up, down = call(
        reduce_kernel,
        "reduce",
        (shape(3 * BOX_DEV, 128), shape(32, 128), shape(32, 128)),
        [("v", nodes), ("v", own)] + [("v", r) for r in around(own)],
    )
    low = lax.ppermute(up, "vol", [(i, i + 1) for i in range(31)])
    high = lax.ppermute(down, "vol", [(i + 1, i) for i in range(31)])
    near, codes = neighbours.T, faces.transpose(1, 0, 2)
    velocity, inner = call(
        inner_kernel,
        "inner",
        (shape(3, BOX_DEV, 128), shape(BOX_DEV, 256)),
        [("s", where), ("s", near), ("v", nodes), ("v", d), ("v", codes)],
        [
            pltpu.VMEM((8 * BOX_DEV, 128), F),
            pltpu.VMEM((3, 16 * BOX_DEV, 128), F),
            pltpu.VMEM((6 * BOX_DEV, 128), I),
        ],
        us=6,
    )
    (swept,) = call(
        edge_kernel,
        "edges",
        (shape(BOX_DEV, 256),),
        [("s", where), ("s", near), ("v", nodes), ("v", d), ("v", low), ("v", high), ("v", codes), ("v", inner)],
        [
            pltpu.VMEM((8 * NEAR, 128), F),
            pltpu.VMEM((3, 128, 128), F),
            pltpu.VMEM((6 * BOX_DEV, 128), I),
        ],
    )
    return velocity.transpose(1, 0, 2), swept


def solution(mesh):
    placed = (
        P("vol", None, None),
        P(("vol", "surf"), None, None),
        P(("vol", "surf"), None, None),
        P(("vol", "surf"), None),
        P("surf", "vol", None),
        P("vol", None),
        P("vol", None, None),
    )
    return jax.shard_map(
        body,
        mesh=mesh,
        in_specs=placed,
        out_specs=(P("vol", None, None), P("vol", None)),
        check_vma=False,
    )
```

```python
import functools

import jax
import jax.numpy as jnp
from jax import lax
from jax.experimental import pallas as pl
from jax.experimental.pallas import tpu as pltpu
from jax.sharding import PartitionSpec as P

BF = jnp.bfloat16
F = jnp.float32
I = jnp.int32
BOTH = ("vol", "surf")
DEVICES = 128
SLOTS = 8
ASK = 3 * SLOTS + 1
GIVE = 3 * SLOTS
UNROLL = 8
BOX_DEV = 64
HALO = 4
NEAR = BOX_DEV + 2 * HALO
TINY = 1e-30
VMEM = pl.BlockSpec(memory_space=pltpu.VMEM)
SMEM = pl.BlockSpec(memory_space=pltpu.SMEM)
FAR = pl.BlockSpec(memory_space=pltpu.HBM)
SPACES = {"v": VMEM, "s": SMEM, "f": FAR}


def call(kernel, name, outs, ins, scratch=(), mib=8, us=2):
    specs = [SPACES[space] for space, _ in ins]
    return pl.pallas_call(
        kernel,
        name=name,
        out_shape=outs,
        in_specs=specs,
        out_specs=tuple(VMEM for _ in outs),
        scratch_shapes=list(scratch),
        compiler_params=pltpu.CompilerParams(vmem_limit_bytes=mib << 20),
        cost_estimate=pl.CostEstimate(flops=us * 10**9, bytes_accessed=us * 10**6, transcendentals=0),
    )(*[array for _, array in ins])


def split3(x):
    first = x.astype(BF).astype(F)
    rest = x - first
    second = rest.astype(BF).astype(F)
    return first, second, (rest - second).astype(BF).astype(F)


def slot_table(listed):
    listed = listed.astype(F).T.astype(I)
    owner = listed >> 6
    local = (listed & 63) + 1
    lanes = lax.broadcasted_iota(I, (BOX_DEV, DEVICES), 1)
    table = jnp.zeros((BOX_DEV, DEVICES), I)
    for k in range(listed.shape[1]):
        hit = owner[:, k : k + 1] == lanes
        table = jnp.where(hit, local[:, k : k + 1], table)
    table = table.astype(F)
    used = table > 0.0
    row = lax.broadcasted_iota(I, (BOX_DEV, BOX_DEV), 0)
    col = lax.broadcasted_iota(I, (BOX_DEV, BOX_DEV), 1)
    before = (col < row).astype(F).astype(BF)
    rank = jnp.dot(before, used.astype(F).astype(BF), preferred_element_type=F)
    return table, jnp.where(used, rank, -1.0)


def prep_kernel(list_ref, node_ref, o_ref):
    table, slot = slot_table(list_ref[...])
    slot_t = slot.T
    nodes = jnp.concatenate([node_ref[c] for c in range(3)], 1)
    parts = [p.astype(BF) for p in split3(nodes)]
    ids = []
    for j in range(SLOTS):
        at = float(j)
        ids.append(jnp.sum(jnp.where(slot == at, table - 1.0, 0.0), axis=0, keepdims=True))
        sel = (slot_t == at).astype(F).astype(BF)
        got = sum(jnp.dot(sel, p, preferred_element_type=F) for p in parts)
        for c in range(3):
            o_ref[pl.ds(c * SLOTS + j, DEVICES, stride=ASK), :] = got[:, c * 128 : (c + 1) * 128]
    stacked = jnp.concatenate(ids + [jnp.zeros((128 - SLOTS, 128), F)], 0).T
    o_ref[pl.ds(ASK - 1, DEVICES, stride=ASK), :] = stacked


def feat_kernel(where_ref, own_ref, one_ref, two_ref, three_ref, a_ref, cf_ref):
    for k, ref in enumerate((own_ref, one_ref, two_ref, three_ref)):
        first = ((where_ref[1] + 4 - k) & 3) * BOX_DEV

        def some(h, carry):
            base = pl.multiple_of(h * 8, 8)
            x, y, z, r, kx, ky, kz = [ref[pl.ds(c * BOX_DEV + base, 8), :] for c in range(7)]
            inv = 1.0 / (r * r)
            scale = -2.0 * inv
            rows = [x * scale, y * scale, z * scale, inv, inv * (x * x + y * y + z * z)]
            rows = [split3(t) for t in rows]
            ks = [split3(4.0 * t) for t in (kx, ky, kz)]
            for u in range(8):
                def part(n):
                    return [t[n][u : u + 1] for t in rows] + [jnp.zeros((3, 128), F)]

                p, q, t = part(0), part(1), part(2)
                s = jnp.concatenate(p * 3 + q * 2 + t, 0).astype(BF)
                at = first + base + u
                a_ref[pl.ds(pl.multiple_of(at * 48, 16), 48), :] = s
                c = jnp.concatenate(
                    [t[n][u : u + 1] for n in range(2) for t in ks] + [jnp.zeros((10, 128), F)], 0
                ).astype(BF)
                cf_ref[pl.ds(pl.multiple_of(at * 16, 16), 16), :] = c
            return carry

        lax.fori_loop(0, BOX_DEV // 8, some, 0)


def terms_kernel(
    x_ref, far_ref, farc_ref, o_ref, a_ref, cf_ref, v_ref, b_ref, q_ref, w_ref, r_ref, stage_ref, ids_ref, sem, a_sem, c_sem
):
    a_copy = pltpu.make_async_copy(far_ref, a_ref, a_sem)
    c_copy = pltpu.make_async_copy(farc_ref, cf_ref, c_sem)
    a_copy.start()
    c_copy.start()
    stage_ref[...] = x_ref[pl.ds(ASK - 1, DEVICES, stride=ASK), :].T[0:SLOTS].astype(I)
    copy = pltpu.make_async_copy(stage_ref, ids_ref, sem)
    copy.start()
    for buf in range(2):
        for k in range(3):
            v_ref[buf, k, pl.ds(32, 32), :] = jnp.zeros((32, 128), F)
        v_ref[buf, 0, pl.ds(32, 8), :] = jnp.ones((8, 128), F)
    copy.wait()

    def stage0(i, buf):
        i = jnp.minimum(i, DEVICES - 1)
        base = i * ASK
        x, y, z = [x_ref[pl.ds(base + c * SLOTS, SLOTS), :] for c in range(3)]
        for f, value in enumerate((x, y, z, x * x + y * y + z * z)):
            first = value.astype(BF).astype(F)
            rest = value - first
            second = rest.astype(BF).astype(F)
            for k, part in enumerate((first, second, rest - second)):
                v_ref[buf, k, pl.ds(f * 8, 8), :] = part
        for j in range(SLOTS):
            v = [v_ref[buf, k, pl.ds(j, 8, stride=8), :] for k in range(3)]
            b_ref[buf, j] = jnp.concatenate(
                [v[0], v[1], v[2], v[0], v[1], v[0]], 0
            ).astype(BF)

    def stage1(i, buf, j):
        i = jnp.minimum(i, DEVICES - 1)
        g = (i & 3) * BOX_DEV + ids_ref[j, i]
        a = a_ref[pl.ds(pl.multiple_of(g * 48, 16), 48), :]
        q_ref[buf, j] = lax.dot_general(
            a, b_ref[buf, j], (((0,), (0,)), ((), ())), preferred_element_type=F
        )

    def stage2(buf, j):
        m = jnp.maximum(q_ref[buf, j], TINY)
        q = m * lax.rsqrt(m)
        t = jnp.maximum(1.0 - q, 0.0)
        t = t * t
        w = (t * t) * (q + 0.25)
        high = w.astype(BF)
        w_ref[buf, j, 0:128, :] = high
        w_ref[buf, j, 128:256, :] = (w - high.astype(F)).astype(BF)

    def stage3(i, buf, j):
        g = (i & 3) * BOX_DEV + ids_ref[j, i]
        c = cf_ref[pl.ds(pl.multiple_of(g * 16, 16), 16), :]
        c = jnp.concatenate([c, c], 1)
        r = jnp.dot(c, w_ref[buf, j], preferred_element_type=F)
        r_ref[buf, pl.ds(j, 6, stride=SLOTS), :] = r[0:6]

    def stage4(i, buf):
        base = pl.multiple_of(i * GIVE, GIVE)
        o_ref[pl.ds(base, GIVE), :] = r_ref[buf, 0:GIVE, :] + r_ref[buf, GIVE : 2 * GIVE, :]

    slots = range(SLOTS)
    stage0(0, 0)
    stage0(1, 1)
    a_copy.wait()
    c_copy.wait()
    for j in slots:
        stage1(0, 0, j)
    stage0(2, 0)
    for j in slots:
        stage1(1, 1, j)
    for j in slots:
        stage2(0, j)

    def some(h, carry):
        for u in range(UNROLL):
            i = h * UNROLL + u
            buf = u % 2
            for j in slots:
                stage1(i + 2, buf, j)
                stage2(1 - buf, j)
                stage3(i, buf, j)
            stage4(i, buf)
            stage0(i + 3, 1 - buf)
        return carry

    lax.fori_loop(0, DEVICES // UNROLL, some, 0)


def sum_kernel(list_ref, back_ref, o_ref):
    _, slot = slot_table(list_ref[...])
    acc = jnp.zeros((BOX_DEV, 384), F)
    for j in range(SLOTS):
        sel = (slot == float(j)).astype(F).astype(BF)
        terms = jnp.concatenate(
            [back_ref[pl.ds(c * SLOTS + j, DEVICES, stride=GIVE), :] for c in range(3)], 1
        )
        for part in split3(terms):
            acc = acc + jnp.dot(sel, part.astype(BF), preferred_element_type=F)
    for c in range(3):
        o_ref[c * BOX_DEV : (c + 1) * BOX_DEV, :] = acc[:, c * 128 : (c + 1) * 128]


def reduce_kernel(node_ref, own_ref, one_ref, two_ref, three_ref, d_ref, up_ref, down_ref):
    d_ref[...] = own_ref[...] + one_ref[...] + two_ref[...] + three_ref[...]
    zero = jnp.zeros((HALO, 128), F)
    x = [node_ref[c] for c in range(3)]
    d = [d_ref[c * BOX_DEV : (c + 1) * BOX_DEV, :] for c in range(3)]
    for ref, first in ((up_ref, BOX_DEV - HALO), (down_ref, 0)):
        ref[...] = jnp.concatenate([t[first : first + HALO] for t in x + d] + [zero, zero], 0)


def corners(near_ref, tab_ref, code_ref, cor_ref, box, at, origin, count):
    tables = []
    for j in range(8):
        row = near_ref[j, box] - origin
        tables.append(tab_ref[pl.ds(pl.multiple_of(row * 8, 8), 8), :])
    for h in range(2):
        for k in range(3):
            code = code_ref[pl.ds((k * 2 + h) * BOX_DEV + box, 1), :]
            code = jnp.broadcast_to(code, (8, 128))
            lane = code & 127
            which = code >> 7
            got = None
            for j in range(8):
                value = jnp.take_along_axis(tables[j], lane, axis=1)
                got = value if got is None else jnp.where(which == j, value, got)
            cor_ref[k, pl.ds(h * count + at, 8, stride=2 * count), :] = got


def volumes(refs, h, count):
    def corner(k):
        part = [ref[k, pl.ds((c * 2 + h) * count, count), :] for ref in refs for c in range(6 // len(refs))]
        return [part[c] + 0.5 * part[c + 3] for c in range(3)], part[3:6]

    (ma, da), (mb, db), (mc, dc) = corner(0), corner(1), corner(2)
    u = [mb[c] - ma[c] for c in range(3)]
    w = [mc[c] - ma[c] for c in range(3)]
    swept = None
    for c in range(3):
        p, q = (c + 1) % 3, (c + 2) % 3
        normal = 0.5 * (u[p] * w[q] - u[q] * w[p])
        term = ((da[c] + db[c] + dc[c]) / 3.0) * normal
        swept = term if swept is None else swept + term
    return swept


def split_codes(face_ref, code_ref):
    for k in range(3):
        for h in range(2):
            code_ref[pl.ds((k * 2 + h) * BOX_DEV, BOX_DEV), :] = face_ref[
                k, :, h * 128 : (h + 1) * 128
            ]


def gather_three(near_ref, face_ref, rows, origin, put, tab_ref, code_ref):
    zero = jnp.zeros((BOX_DEV, 128), F)
    for half in range(2):
        for c in range(4):
            tab_ref[pl.ds(half * 4 + c, BOX_DEV, stride=8), :] = rows[c] if c < 3 else zero
    split_codes(face_ref, code_ref)
    upper = lax.broadcasted_iota(I, (8, 128), 0) >= 4

    def some(g, carry):
        for u in range(8):
            box = g * 8 + HALO + u
            tables = []
            for j in range(8):
                row = near_ref[j, box] - origin
                tables.append(tab_ref[pl.ds(pl.multiple_of(row * 8, 8), 8), :])
            tables = [jnp.where(upper, tables[j + 4], tables[j]) for j in range(4)]
            for h in range(2):
                for k in range(3):
                    code = code_ref[pl.ds((k * 2 + h) * BOX_DEV + box, 1), :]
                    code = jnp.broadcast_to(code, (8, 128))
                    lane = code & 127
                    which = (code >> 7) & 3
                    got = None
                    for j in range(4):
                        value = jnp.take_along_axis(tables[j], lane, axis=1)
                        got = value if got is None else jnp.where(which == j, value, got)
                    got = jnp.where(code >= 512, pltpu.roll(got, 4, 0), got)
                    put[k, pl.ds(h * BOX_DEV + box, 3, stride=2 * BOX_DEV), :] = got[0:3]
        return carry

    lax.fori_loop(0, (BOX_DEV - 2 * HALO) // 8, some, 0)


def place_kernel(where_ref, near_ref, node_ref, face_ref, o_ref, tab_ref, code_ref):
    rows = [node_ref[c] for c in range(3)]
    gather_three(near_ref, face_ref, rows, where_ref[0] * BOX_DEV, o_ref, tab_ref, code_ref)


def inner_kernel(where_ref, near_ref, d_ref, place_ref, face_ref, v_ref, s_ref, tab_ref, cor_ref, code_ref):
    rows = [d_ref[c * BOX_DEV : (c + 1) * BOX_DEV, :] for c in range(3)]
    gather_three(near_ref, face_ref, rows, where_ref[0] * BOX_DEV, cor_ref, tab_ref, code_ref)
    for h in range(2):
        s_ref[:, h * 128 : (h + 1) * 128] = volumes((place_ref, cor_ref), h, BOX_DEV)
    for c in range(3):
        v_ref[c] = d_ref[c * BOX_DEV : (c + 1) * BOX_DEV, :] * 2.0


def edge_kernel(
    where_ref, near_ref, node_ref, d_ref, low_ref, high_ref, face_ref, in_ref, s_ref, tab_ref, cor_ref, code_ref
):
    for c in range(6):
        own = node_ref[c] if c < 3 else d_ref[(c - 3) * BOX_DEV : (c - 2) * BOX_DEV, :]
        edge = slice(c * HALO, (c + 1) * HALO)
        tab_ref[pl.ds(c, NEAR, stride=8), :] = jnp.concatenate(
            [low_ref[edge, :], own, high_ref[edge, :]], 0
        )
    for c in (6, 7):
        tab_ref[pl.ds(c, NEAR, stride=8), :] = jnp.zeros((NEAR, 128), F)
    split_codes(face_ref, code_ref)
    origin = where_ref[0] * BOX_DEV - HALO
    for at in range(2 * HALO):
        box = at if at < HALO else BOX_DEV - 2 * HALO + at
        corners(near_ref, tab_ref, code_ref, cor_ref, box, at, origin, 2 * HALO)
    s_ref[...] = in_ref[...]
    for h in range(2):
        swept = volumes((cor_ref,), h, 2 * HALO)
        s_ref[0:HALO, h * 128 : (h + 1) * 128] = swept[0:HALO]
        s_ref[BOX_DEV - HALO : BOX_DEV, h * 128 : (h + 1) * 128] = swept[HALO:]


def to_all(array):
    peers = DEVICES // 4
    rows = array.shape[0] // peers
    packets = array.reshape(peers, rows, 1, 128)
    packets = lax.all_to_all(packets, "vol", split_axis=0, concat_axis=0, tiled=True)
    return packets.reshape(peers * rows, 128)


def around(array):
    return [lax.ppermute(array, "surf", [(i, (i + k) % 4) for i in range(4)]) for k in (1, 2, 3)]


def shape(*dims, kind=F):
    return jax.ShapeDtypeStruct(dims, kind)


def body(node_pos, centres, coefs, radii, block_list, neighbours, faces):
    listed = block_list[0].T
    nodes, cens, weights = [a.transpose(1, 0, 2) for a in (node_pos, centres, coefs)]
    where = jnp.stack([lax.axis_index("vol"), lax.axis_index("surf")]).astype(I)
    blocks = jnp.concatenate(
        [cens.reshape(3 * BOX_DEV, 128), radii, weights.reshape(3 * BOX_DEV, 128)], 0
    )
    (sent,) = call(
        prep_kernel,
        "prep",
        (shape(DEVICES * ASK, 128),),
        [("v", listed), ("v", nodes)],
    )
    near, codes = neighbours.T, faces.transpose(1, 0, 2)
    sent, early = lax.optimization_barrier((sent, codes))
    (place,) = call(
        place_kernel,
        "place",
        (shape(3, 6 * BOX_DEV, 128),),
        [("s", where), ("s", near), ("v", nodes), ("v", early)],
        [pltpu.VMEM((8 * BOX_DEV, 128), F), pltpu.VMEM((6 * BOX_DEV, 128), I)],
        us=4,
    )
    tables = call(
        feat_kernel,
        "feats",
        (shape(4 * BOX_DEV * 48, 128, kind=BF), shape(4 * BOX_DEV * 16, 128, kind=BF)),
        [("s", where), ("v", blocks)] + [("v", r) for r in around(blocks)],
        us=5,
    )
    (terms,) = call(
        terms_kernel,
        "terms",
        (shape(DEVICES * GIVE, 128),),
        [("v", to_all(sent))] + [("f", pltpu.with_memory_space_constraint(t, pltpu.HBM)) for t in tables],
        [
            pltpu.VMEM((4 * BOX_DEV * 48, 128), BF),
            pltpu.VMEM((4 * BOX_DEV * 16, 128), BF),
            pltpu.VMEM((2, 3, 64, 128), F),
            pltpu.VMEM((2, SLOTS, 48, 128), BF),
            pltpu.VMEM((2, SLOTS, 128, 128), F),
            pltpu.VMEM((2, SLOTS, 256, 128), BF),
            pltpu.VMEM((2, 2 * GIVE, 128), F),
            pltpu.VMEM((SLOTS, 128), I),
            pltpu.SMEM((SLOTS, 128), I),
            pltpu.SemaphoreType.DMA,
            pltpu.SemaphoreType.DMA,
            pltpu.SemaphoreType.DMA,
        ],
        mib=16,
        us=45,
    )
    (own,) = call(
        sum_kernel,
        "sums",
        (shape(3 * BOX_DEV, 128),),
        [("v", listed), ("v", to_all(terms))],
    )
    d, up, down = call(
        reduce_kernel,
        "reduce",
        (shape(3 * BOX_DEV, 128), shape(32, 128), shape(32, 128)),
        [("v", nodes), ("v", own)] + [("v", r) for r in around(own)],
    )
    low = lax.ppermute(up, "vol", [(i, i + 1) for i in range(31)])
    high = lax.ppermute(down, "vol", [(i + 1, i) for i in range(31)])
    velocity, inner = call(
        inner_kernel,
        "inner",
        (shape(3, BOX_DEV, 128), shape(BOX_DEV, 256)),
        [("s", where), ("s", near), ("v", d), ("v", place), ("v", codes)],
        [
            pltpu.VMEM((8 * BOX_DEV, 128), F),
            pltpu.VMEM((3, 6 * BOX_DEV, 128), F),
            pltpu.VMEM((6 * BOX_DEV, 128), I),
        ],
        us=4,
    )
    (swept,) = call(
        edge_kernel,
        "edges",
        (shape(BOX_DEV, 256),),
        [("s", where), ("s", near), ("v", nodes), ("v", d), ("v", low), ("v", high), ("v", codes), ("v", inner)],
        [
            pltpu.VMEM((8 * NEAR, 128), F),
            pltpu.VMEM((3, 128, 128), F),
            pltpu.VMEM((6 * BOX_DEV, 128), I),
        ],
    )
    return velocity.transpose(1, 0, 2), swept


def solution(mesh):
    placed = (
        P("vol", None, None),
        P(("vol", "surf"), None, None),
        P(("vol", "surf"), None, None),
        P(("vol", "surf"), None),
        P("surf", "vol", None),
        P("vol", None),
        P("vol", None, None),
    )
    return jax.shard_map(
        body,
        mesh=mesh,
        in_specs=placed,
        out_specs=(P("vol", None, None), P("vol", None)),
        check_vma=False,
    )
```

```python
import functools

import jax
import jax.numpy as jnp
from jax import lax
from jax.experimental import pallas as pl
from jax.experimental.pallas import tpu as pltpu
from jax.sharding import PartitionSpec as P

BF = jnp.bfloat16
F = jnp.float32
I = jnp.int32
BOTH = ("vol", "surf")
DEVICES = 128
SLOTS = 8
ASK = 3 * SLOTS + 1
GIVE = 3 * SLOTS
FEATS = 32
UNROLL = 8
BOX_DEV = 64
HALO = 4
NEAR = BOX_DEV + 2 * HALO
TINY = 1e-30
VMEM = pl.BlockSpec(memory_space=pltpu.VMEM)
SMEM = pl.BlockSpec(memory_space=pltpu.SMEM)
FAR = pl.BlockSpec(memory_space=pltpu.HBM)
SPACES = {"v": VMEM, "s": SMEM, "f": FAR}


def call(kernel, name, outs, ins, scratch=(), mib=8, us=2, out=VMEM):
    specs = [SPACES[space] for space, _ in ins]
    return pl.pallas_call(
        kernel,
        name=name,
        out_shape=outs,
        in_specs=specs,
        out_specs=tuple(out for _ in outs),
        scratch_shapes=list(scratch),
        compiler_params=pltpu.CompilerParams(vmem_limit_bytes=mib << 20),
        cost_estimate=pl.CostEstimate(flops=us * 10**9, bytes_accessed=us * 10**6, transcendentals=0),
    )(*[array for _, array in ins])


def split3(x):
    first = x.astype(BF).astype(F)
    rest = x - first
    second = rest.astype(BF).astype(F)
    return first, second, (rest - second).astype(BF).astype(F)


def slot_table(listed):
    listed = listed.astype(F).T.astype(I)
    owner = listed >> 6
    local = (listed & 63) + 1
    lanes = lax.broadcasted_iota(I, (BOX_DEV, DEVICES), 1)
    table = jnp.zeros((BOX_DEV, DEVICES), I)
    for k in range(listed.shape[1]):
        hit = owner[:, k : k + 1] == lanes
        table = jnp.where(hit, local[:, k : k + 1], table)
    table = table.astype(F)
    used = table > 0.0
    row = lax.broadcasted_iota(I, (BOX_DEV, BOX_DEV), 0)
    col = lax.broadcasted_iota(I, (BOX_DEV, BOX_DEV), 1)
    before = (col < row).astype(F).astype(BF)
    rank = jnp.dot(before, used.astype(F).astype(BF), preferred_element_type=F)
    return table, jnp.where(used, rank, -1.0)


def prep_kernel(list_ref, node_ref, o_ref):
    table, slot = slot_table(list_ref[...])
    slot_t = slot.T
    nodes = jnp.concatenate([node_ref[c] for c in range(3)], 1)
    parts = [p.astype(BF) for p in split3(nodes)]
    ids = []
    for j in range(SLOTS):
        at = float(j)
        ids.append(jnp.sum(jnp.where(slot == at, table - 1.0, 0.0), axis=0, keepdims=True))
        sel = (slot_t == at).astype(F).astype(BF)
        got = sum(jnp.dot(sel, p, preferred_element_type=F) for p in parts)
        for c in range(3):
            o_ref[pl.ds(c * SLOTS + j, DEVICES, stride=ASK), :] = got[:, c * 128 : (c + 1) * 128]
    stacked = jnp.concatenate(ids + [jnp.zeros((128 - SLOTS, 128), F)], 0).T
    o_ref[pl.ds(ASK - 1, DEVICES, stride=ASK), :] = stacked


def feat_kernel(own_ref, one_ref, two_ref, three_ref, far_ref, farc_ref, a_ref, cf_ref, sems):
    copies = []
    for k, ref in enumerate((own_ref, one_ref, two_ref, three_ref)):
        first = k * BOX_DEV

        def some(h, carry):
            base = pl.multiple_of(h * 8, 8)
            x, y, z, r, kx, ky, kz = [ref[pl.ds(c * BOX_DEV + base, 8), :] for c in range(7)]
            inv = 1.0 / (r * r)
            scale = -2.0 * inv
            rows = [x * scale, y * scale, z * scale, inv, inv * (x * x + y * y + z * z)]
            rows = [split3(t) for t in rows]
            ks = [split3(4.0 * t) for t in (kx, ky, kz)]
            for u in range(8):
                s = [t[n][u : u + 1] for t in rows[0:4] for n in (0, 0, 0, 1, 1, 2)]
                s += [rows[4][n][u : u + 1] for n in range(3)] + [jnp.zeros((5, 128), F)]
                at = first + base + u
                a_ref[pl.ds(pl.multiple_of(at * FEATS, FEATS), FEATS), :] = jnp.concatenate(s, 0).astype(BF)
                c = jnp.concatenate(
                    [t[n][u : u + 1] for n in range(2) for t in ks] + [jnp.zeros((10, 128), F)], 0
                ).astype(BF)
                cf_ref[pl.ds(pl.multiple_of(at * 16, 16), 16), :] = c
            return carry

        lax.fori_loop(0, BOX_DEV // 8, some, 0)
        for n, (near, far, height) in enumerate(((a_ref, far_ref, FEATS), (cf_ref, farc_ref, 16))):
            part = pl.ds(first * height, BOX_DEV * height)
            copy = pltpu.make_async_copy(near.at[part, :], far.at[part, :], sems.at[2 * k + n])
            copy.start()
            copies.append(copy)
    for copy in copies:
        copy.wait()


def terms_kernel(
    where_ref, x_ref, far_ref, farc_ref, o_ref, a_ref, cf_ref, v_ref, b_ref, q_ref, w_ref, r_ref, stage_ref, ids_ref, sem, a_sem, c_sem
):
    a_copy = pltpu.make_async_copy(far_ref, a_ref, a_sem)
    c_copy = pltpu.make_async_copy(farc_ref, cf_ref, c_sem)
    a_copy.start()
    c_copy.start()
    stage_ref[...] = x_ref[pl.ds(ASK - 1, DEVICES, stride=ASK), :].T[0:SLOTS].astype(I)
    copy = pltpu.make_async_copy(stage_ref, ids_ref, sem)
    copy.start()
    for buf in range(2):
        v_ref[buf, pl.ds(192, 24), :] = jnp.ones((24, 128), F)
        v_ref[buf, pl.ds(216, 40), :] = jnp.zeros((40, 128), F)
    copy.wait()
    surf = where_ref[1]

    def stage0(i, buf):
        i = jnp.minimum(i, DEVICES - 1)
        base = i * ASK
        x, y, z = [x_ref[pl.ds(base + c * SLOTS, SLOTS), :] for c in range(3)]
        for f, value in enumerate((x, y, z, x * x + y * y + z * z)):
            first = value.astype(BF).astype(F)
            rest = value - first
            second = rest.astype(BF).astype(F)
            third = rest - second
            for k, part in enumerate((first, second, third, first, second, first)):
                v_ref[buf, pl.ds((f * 6 + k) * 8, 8), :] = part
        for j in range(SLOTS):
            v = [v_ref[buf, pl.ds(n * 64 + j, 8, stride=8), :] for n in range(4)]
            b_ref[buf, j] = jnp.concatenate(v, 0).astype(BF)

    def stage1(i, buf, j):
        i = jnp.minimum(i, DEVICES - 1)
        g = ((surf - i) & 3) * BOX_DEV + ids_ref[j, i]
        a = a_ref[pl.ds(pl.multiple_of(g * FEATS, FEATS), FEATS), :]
        q_ref[buf, j] = lax.dot_general(
            a, b_ref[buf, j], (((0,), (0,)), ((), ())), preferred_element_type=F
        )

    def stage2(buf, j):
        m = jnp.maximum(q_ref[buf, j], TINY)
        q = m * lax.rsqrt(m)
        t = jnp.maximum(1.0 - q, 0.0)
        t = t * t
        w = (t * t) * (q + 0.25)
        high = w.astype(BF)
        w_ref[buf, j, 0:128, :] = high
        w_ref[buf, j, 128:256, :] = (w - high.astype(F)).astype(BF)

    def stage3(i, buf, j):
        g = ((surf - i) & 3) * BOX_DEV + ids_ref[j, i]
        c = cf_ref[pl.ds(pl.multiple_of(g * 16, 16), 16), :]
        c = jnp.concatenate([c, c], 1)
        r = jnp.dot(c, w_ref[buf, j], preferred_element_type=F)
        r_ref[buf, pl.ds(j, 6, stride=SLOTS), :] = r[0:6]

    def stage4(i, buf):
        base = pl.multiple_of(i * GIVE, GIVE)
        o_ref[pl.ds(base, GIVE), :] = r_ref[buf, 0:GIVE, :] + r_ref[buf, GIVE : 2 * GIVE, :]

    slots = range(SLOTS)
    stage0(0, 0)
    stage0(1, 1)
    a_copy.wait()
    c_copy.wait()
    for j in slots:
        stage1(0, 0, j)
    stage0(2, 0)
    for j in slots:
        stage1(1, 1, j)
    for j in slots:
        stage2(0, j)

    def some(h, carry):
        for u in range(UNROLL):
            i = h * UNROLL + u
            buf = u % 2
            for j in slots:
                stage1(i + 2, buf, j)
                stage2(1 - buf, j)
                stage3(i, buf, j)
            stage4(i, buf)
            stage0(i + 3, 1 - buf)
        return carry

    lax.fori_loop(0, DEVICES // UNROLL, some, 0)


def sum_kernel(list_ref, back_ref, o_ref):
    _, slot = slot_table(list_ref[...])
    acc = jnp.zeros((BOX_DEV, 384), F)
    for j in range(SLOTS):
        sel = (slot == float(j)).astype(F).astype(BF)
        terms = jnp.concatenate(
            [back_ref[pl.ds(c * SLOTS + j, DEVICES, stride=GIVE), :] for c in range(3)], 1
        )
        for part in split3(terms):
            acc = acc + jnp.dot(sel, part.astype(BF), preferred_element_type=F)
    for c in range(3):
        o_ref[c * BOX_DEV : (c + 1) * BOX_DEV, :] = acc[:, c * 128 : (c + 1) * 128]


def reduce_kernel(node_ref, own_ref, one_ref, two_ref, three_ref, d_ref, up_ref, down_ref):
    d_ref[...] = own_ref[...] + one_ref[...] + two_ref[...] + three_ref[...]
    zero = jnp.zeros((HALO, 128), F)
    x = [node_ref[c] for c in range(3)]
    d = [d_ref[c * BOX_DEV : (c + 1) * BOX_DEV, :] for c in range(3)]
    for ref, first in ((up_ref, BOX_DEV - HALO), (down_ref, 0)):
        ref[...] = jnp.concatenate([t[first : first + HALO] for t in x + d] + [zero, zero], 0)


def corners(near_ref, tab_ref, code_ref, cor_ref, box, at, origin, count):
    tables = []
    for j in range(8):
        row = near_ref[j, box] - origin
        tables.append(tab_ref[pl.ds(pl.multiple_of(row * 8, 8), 8), :])
    for h in range(2):
        for k in range(3):
            code = code_ref[pl.ds((k * 2 + h) * BOX_DEV + box, 1), :]
            code = jnp.broadcast_to(code, (8, 128))
            lane = code & 127
            which = code >> 7
            got = None
            for j in range(8):
                value = jnp.take_along_axis(tables[j], lane, axis=1)
                got = value if got is None else jnp.where(which == j, value, got)
            cor_ref[k, pl.ds(h * count + at, 8, stride=2 * count), :] = got


def volumes(refs, h, count):
    def corner(k):
        part = [ref[k, pl.ds((c * 2 + h) * count, count), :] for ref in refs for c in range(6 // len(refs))]
        return [part[c] + 0.5 * part[c + 3] for c in range(3)], part[3:6]

    (ma, da), (mb, db), (mc, dc) = corner(0), corner(1), corner(2)
    u = [mb[c] - ma[c] for c in range(3)]
    w = [mc[c] - ma[c] for c in range(3)]
    swept = None
    for c in range(3):
        p, q = (c + 1) % 3, (c + 2) % 3
        normal = 0.5 * (u[p] * w[q] - u[q] * w[p])
        term = ((da[c] + db[c] + dc[c]) / 3.0) * normal
        swept = term if swept is None else swept + term
    return swept


def split_codes(face_ref, code_ref):
    for k in range(3):
        for h in range(2):
            code_ref[pl.ds((k * 2 + h) * BOX_DEV, BOX_DEV), :] = face_ref[
                k, :, h * 128 : (h + 1) * 128
            ]


def gather_three(near_ref, face_ref, rows, origin, put, tab_ref, code_ref):
    zero = jnp.zeros((BOX_DEV, 128), F)
    for half in range(2):
        for c in range(4):
            tab_ref[pl.ds(half * 4 + c, BOX_DEV, stride=8), :] = rows[c] if c < 3 else zero
    split_codes(face_ref, code_ref)
    upper = lax.broadcasted_iota(I, (8, 128), 0) >= 4

    def some(g, carry):
        for u in range(8):
            box = g * 8 + HALO + u
            tables = []
            for j in range(8):
                row = near_ref[j, box] - origin
                tables.append(tab_ref[pl.ds(pl.multiple_of(row * 8, 8), 8), :])
            tables = [jnp.where(upper, tables[j + 4], tables[j]) for j in range(4)]
            for h in range(2):
                for k in range(3):
                    code = code_ref[pl.ds((k * 2 + h) * BOX_DEV + box, 1), :]
                    code = jnp.broadcast_to(code, (8, 128))
                    lane = code & 127
                    which = (code >> 7) & 3
                    got = None
                    for j in range(4):
                        value = jnp.take_along_axis(tables[j], lane, axis=1)
                        got = value if got is None else jnp.where(which == j, value, got)
                    got = jnp.where(code >= 512, pltpu.roll(got, 4, 0), got)
                    put[k, pl.ds(h * BOX_DEV + box, 3, stride=2 * BOX_DEV), :] = got[0:3]
        return carry

    lax.fori_loop(0, (BOX_DEV - 2 * HALO) // 8, some, 0)


def place_kernel(where_ref, near_ref, node_ref, face_ref, o_ref, tab_ref, code_ref):
    rows = [node_ref[c] for c in range(3)]
    gather_three(near_ref, face_ref, rows, where_ref[0] * BOX_DEV, o_ref, tab_ref, code_ref)


def inner_kernel(where_ref, near_ref, d_ref, place_ref, face_ref, v_ref, s_ref, tab_ref, cor_ref, code_ref):
    rows = [d_ref[c * BOX_DEV : (c + 1) * BOX_DEV, :] for c in range(3)]
    gather_three(near_ref, face_ref, rows, where_ref[0] * BOX_DEV, cor_ref, tab_ref, code_ref)
    for h in range(2):
        s_ref[:, h * 128 : (h + 1) * 128] = volumes((place_ref, cor_ref), h, BOX_DEV)
    for c in range(3):
        v_ref[c] = d_ref[c * BOX_DEV : (c + 1) * BOX_DEV, :] * 2.0


def edge_kernel(
    where_ref, near_ref, node_ref, d_ref, low_ref, high_ref, face_ref, in_ref, s_ref, tab_ref, cor_ref, code_ref
):
    for c in range(6):
        own = node_ref[c] if c < 3 else d_ref[(c - 3) * BOX_DEV : (c - 2) * BOX_DEV, :]
        edge = slice(c * HALO, (c + 1) * HALO)
        tab_ref[pl.ds(c, NEAR, stride=8), :] = jnp.concatenate(
            [low_ref[edge, :], own, high_ref[edge, :]], 0
        )
    for c in (6, 7):
        tab_ref[pl.ds(c, NEAR, stride=8), :] = jnp.zeros((NEAR, 128), F)
    split_codes(face_ref, code_ref)
    origin = where_ref[0] * BOX_DEV - HALO
    for at in range(2 * HALO):
        box = at if at < HALO else BOX_DEV - 2 * HALO + at
        corners(near_ref, tab_ref, code_ref, cor_ref, box, at, origin, 2 * HALO)
    s_ref[...] = in_ref[...]
    for h in range(2):
        swept = volumes((cor_ref,), h, 2 * HALO)
        s_ref[0:HALO, h * 128 : (h + 1) * 128] = swept[0:HALO]
        s_ref[BOX_DEV - HALO : BOX_DEV, h * 128 : (h + 1) * 128] = swept[HALO:]


def to_all(array):
    peers = DEVICES // 4
    rows = array.shape[0] // peers
    packets = array.reshape(peers, rows, 1, 128)
    packets = lax.all_to_all(packets, "vol", split_axis=0, concat_axis=0, tiled=True)
    return packets.reshape(peers * rows, 128)


def around(array):
    return [lax.ppermute(array, "surf", [(i, (i + k) % 4) for i in range(4)]) for k in (1, 2, 3)]


def shape(*dims, kind=F):
    return jax.ShapeDtypeStruct(dims, kind)


def body(node_pos, centres, coefs, radii, block_list, neighbours, faces):
    listed = block_list[0].T
    nodes, cens, weights = [a.transpose(1, 0, 2) for a in (node_pos, centres, coefs)]
    where = jnp.stack([lax.axis_index("vol"), lax.axis_index("surf")]).astype(I)
    blocks = jnp.concatenate(
        [cens.reshape(3 * BOX_DEV, 128), radii, weights.reshape(3 * BOX_DEV, 128)], 0
    )
    (sent,) = call(
        prep_kernel,
        "prep",
        (shape(DEVICES * ASK, 128),),
        [("v", listed), ("v", nodes)],
    )
    near, codes = neighbours.T, faces.transpose(1, 0, 2)
    sent, early = lax.optimization_barrier((sent, codes))
    (place,) = call(
        place_kernel,
        "place",
        (shape(3, 6 * BOX_DEV, 128),),
        [("s", where), ("s", near), ("v", nodes), ("v", early)],
        [pltpu.VMEM((8 * BOX_DEV, 128), F), pltpu.VMEM((6 * BOX_DEV, 128), I)],
        us=4,
    )
    sizes = (4 * BOX_DEV * FEATS, 128), (4 * BOX_DEV * 16, 128)
    tables = call(
        feat_kernel,
        "feats",
        tuple(pltpu.HBM(size, BF) for size in sizes),
        [("v", blocks)] + [("v", r) for r in around(blocks)],
        [pltpu.VMEM(size, BF) for size in sizes] + [pltpu.SemaphoreType.DMA((8,))],
        us=5,
        out=FAR,
    )
    (terms,) = call(
        terms_kernel,
        "terms",
        (shape(DEVICES * GIVE, 128),),
        [("s", where), ("v", to_all(sent))] + [("f", pltpu.with_memory_space_constraint(t, pltpu.HBM)) for t in tables],
        [
            pltpu.VMEM((4 * BOX_DEV * FEATS, 128), BF),
            pltpu.VMEM((4 * BOX_DEV * 16, 128), BF),
            pltpu.VMEM((2, 8 * FEATS, 128), F),
            pltpu.VMEM((2, SLOTS, FEATS, 128), BF),
            pltpu.VMEM((2, SLOTS, 128, 128), F),
            pltpu.VMEM((2, SLOTS, 256, 128), BF),
            pltpu.VMEM((2, 2 * GIVE, 128), F),
            pltpu.VMEM((SLOTS, 128), I),
            pltpu.SMEM((SLOTS, 128), I),
            pltpu.SemaphoreType.DMA,
            pltpu.SemaphoreType.DMA,
            pltpu.SemaphoreType.DMA,
        ],
        mib=16,
        us=45,
    )
    (own,) = call(
        sum_kernel,
        "sums",
        (shape(3 * BOX_DEV, 128),),
        [("v", listed), ("v", to_all(terms))],
    )
    d, up, down = call(
        reduce_kernel,
        "reduce",
        (shape(3 * BOX_DEV, 128), shape(32, 128), shape(32, 128)),
        [("v", nodes), ("v", own)] + [("v", r) for r in around(own)],
    )
    low = lax.ppermute(up, "vol", [(i, i + 1) for i in range(31)])
    high = lax.ppermute(down, "vol", [(i + 1, i) for i in range(31)])
    velocity, inner = call(
        inner_kernel,
        "inner",
        (shape(3, BOX_DEV, 128), shape(BOX_DEV, 256)),
        [("s", where), ("s", near), ("v", d), ("v", place), ("v", codes)],
        [
            pltpu.VMEM((8 * BOX_DEV, 128), F),
            pltpu.VMEM((3, 6 * BOX_DEV, 128), F),
            pltpu.VMEM((6 * BOX_DEV, 128), I),
        ],
        us=4,
    )
    (swept,) = call(
        edge_kernel,
        "edges",
        (shape(BOX_DEV, 256),),
        [("s", where), ("s", near), ("v", nodes), ("v", d), ("v", low), ("v", high), ("v", codes), ("v", inner)],
        [
            pltpu.VMEM((8 * NEAR, 128), F),
            pltpu.VMEM((3, 128, 128), F),
            pltpu.VMEM((6 * BOX_DEV, 128), I),
        ],
    )
    return velocity.transpose(1, 0, 2), swept


def solution(mesh):
    placed = (
        P("vol", None, None),
        P(("vol", "surf"), None, None),
        P(("vol", "surf"), None, None),
        P(("vol", "surf"), None),
        P("surf", "vol", None),
        P("vol", None),
        P("vol", None, None),
    )
    return jax.shard_map(
        body,
        mesh=mesh,
        in_specs=placed,
        out_specs=(P("vol", None, None), P("vol", None)),
        check_vma=False,
    )
```

```python
import functools

import jax
import jax.numpy as jnp
from jax import lax
from jax.experimental import pallas as pl
from jax.experimental.pallas import tpu as pltpu
from jax.sharding import PartitionSpec as P

BF = jnp.bfloat16
F = jnp.float32
I = jnp.int32
BOTH = ("vol", "surf")
DEVICES = 128
SLOTS = 8
ASK = 3 * SLOTS + 1
GIVE = 3 * SLOTS
FEATS = 32
UNROLL = 8
BOX_DEV = 64
HALO = 4
NEAR = BOX_DEV + 2 * HALO
TINY = 1e-30
VMEM = pl.BlockSpec(memory_space=pltpu.VMEM)
SMEM = pl.BlockSpec(memory_space=pltpu.SMEM)
FAR = pl.BlockSpec(memory_space=pltpu.HBM)
SPACES = {"v": VMEM, "s": SMEM, "f": FAR}


def call(kernel, name, outs, ins, scratch=(), mib=8, us=2, out=VMEM):
    specs = [SPACES[space] for space, _ in ins]
    return pl.pallas_call(
        kernel,
        name=name,
        out_shape=outs,
        in_specs=specs,
        out_specs=tuple(out for _ in outs),
        scratch_shapes=list(scratch),
        compiler_params=pltpu.CompilerParams(vmem_limit_bytes=mib << 20),
        cost_estimate=pl.CostEstimate(flops=us * 10**9, bytes_accessed=us * 10**6, transcendentals=0),
    )(*[array for _, array in ins])


def split3(x):
    first = x.astype(BF).astype(F)
    rest = x - first
    second = rest.astype(BF).astype(F)
    return first, second, (rest - second).astype(BF).astype(F)


def slot_table(listed):
    listed = listed.astype(F).T.astype(I)
    owner = listed >> 6
    local = (listed & 63) + 1
    lanes = lax.broadcasted_iota(I, (BOX_DEV, DEVICES), 1)
    table = jnp.zeros((BOX_DEV, DEVICES), I)
    for k in range(listed.shape[1]):
        hit = owner[:, k : k + 1] == lanes
        table = jnp.where(hit, local[:, k : k + 1], table)
    table = table.astype(F)
    used = table > 0.0
    row = lax.broadcasted_iota(I, (BOX_DEV, BOX_DEV), 0)
    col = lax.broadcasted_iota(I, (BOX_DEV, BOX_DEV), 1)
    before = (col < row).astype(F).astype(BF)
    rank = jnp.dot(before, used.astype(F).astype(BF), preferred_element_type=F)
    return table, jnp.where(used, rank, -1.0)


def prep_kernel(list_far, node_far, o_far, list_ref, node_ref, low_ref, high_ref, sems):
    list_copy = pltpu.make_async_copy(list_far, list_ref, sems.at[0])
    node_copy = pltpu.make_async_copy(node_far, node_ref, sems.at[1])
    list_copy.start()
    node_copy.start()
    list_copy.wait()
    table, slot = slot_table(list_ref[...])
    slot_t = slot.T
    ids = [
        jnp.sum(jnp.where(slot == float(j), table - 1.0, 0.0), axis=0, keepdims=True)
        for j in range(SLOTS)
    ]
    stacked = jnp.concatenate(ids + [jnp.zeros((128 - SLOTS, 128), F)], 0).T
    node_copy.wait()
    nodes = jnp.concatenate([node_ref[c] for c in range(3)], 1)
    parts = [p.astype(BF) for p in split3(nodes)]
    owners = DEVICES // 2
    copies = []
    for half, ref in enumerate((low_ref, high_ref)):
        rows = slice(half * owners, (half + 1) * owners)
        for j in range(SLOTS):
            sel = (slot_t[rows] == float(j)).astype(F).astype(BF)
            got = sum(jnp.dot(sel, p, preferred_element_type=F) for p in parts)
            for c in range(3):
                ref[pl.ds(c * SLOTS + j, owners, stride=ASK), :] = got[:, c * 128 : (c + 1) * 128]
        ref[pl.ds(ASK - 1, owners, stride=ASK), :] = stacked[rows]
        part = pl.ds(half * owners * ASK, owners * ASK)
        copies.append(pltpu.make_async_copy(ref, o_far.at[part, :], sems.at[2 + half]))
        copies[half].start()
    for copy in copies:
        copy.wait()


def feat_kernel(own_ref, one_ref, two_ref, three_ref, far_ref, farc_ref, a_ref, cf_ref, sems):
    copies = []
    for k, ref in enumerate((own_ref, one_ref, two_ref, three_ref)):
        first = k * BOX_DEV

        def some(h, carry):
            base = pl.multiple_of(h * 8, 8)
            x, y, z, r, kx, ky, kz = [ref[pl.ds(c * BOX_DEV + base, 8), :] for c in range(7)]
            inv = 1.0 / (r * r)
            scale = -2.0 * inv
            rows = [x * scale, y * scale, z * scale, inv, inv * (x * x + y * y + z * z)]
            rows = [split3(t) for t in rows]
            ks = [split3(4.0 * t) for t in (kx, ky, kz)]
            for u in range(8):
                s = [t[n][u : u + 1] for t in rows[0:4] for n in (0, 0, 0, 1, 1, 2)]
                s += [rows[4][n][u : u + 1] for n in range(3)] + [jnp.zeros((5, 128), F)]
                at = first + base + u
                a_ref[pl.ds(pl.multiple_of(at * FEATS, FEATS), FEATS), :] = jnp.concatenate(s, 0).astype(BF)
                c = jnp.concatenate(
                    [t[n][u : u + 1] for n in range(2) for t in ks] + [jnp.zeros((10, 128), F)], 0
                ).astype(BF)
                cf_ref[pl.ds(pl.multiple_of(at * 16, 16), 16), :] = c
            return carry

        lax.fori_loop(0, BOX_DEV // 8, some, 0)
        for n, (near, far, height) in enumerate(((a_ref, far_ref, FEATS), (cf_ref, farc_ref, 16))):
            part = pl.ds(first * height, BOX_DEV * height)
            copy = pltpu.make_async_copy(near.at[part, :], far.at[part, :], sems.at[2 * k + n])
            copy.start()
            copies.append(copy)
    for copy in copies:
        copy.wait()


def terms_kernel(
    where_ref, x_ref, far_ref, farc_ref, o_ref, a_ref, cf_ref, v_ref, b_ref, q_ref, w_ref, r_ref, stage_ref, ids_ref, sem, a_sem, c_sem
):
    a_copy = pltpu.make_async_copy(far_ref, a_ref, a_sem)
    c_copy = pltpu.make_async_copy(farc_ref, cf_ref, c_sem)
    a_copy.start()
    c_copy.start()
    stage_ref[...] = x_ref[pl.ds(ASK - 1, DEVICES, stride=ASK), :].T[0:SLOTS].astype(I)
    copy = pltpu.make_async_copy(stage_ref, ids_ref, sem)
    copy.start()
    for buf in range(2):
        v_ref[buf, pl.ds(192, 24), :] = jnp.ones((24, 128), F)
        v_ref[buf, pl.ds(216, 40), :] = jnp.zeros((40, 128), F)
    copy.wait()
    surf = where_ref[1]

    def stage0(i, buf):
        i = jnp.minimum(i, DEVICES - 1)
        base = i * ASK
        x, y, z = [x_ref[pl.ds(base + c * SLOTS, SLOTS), :] for c in range(3)]
        for f, value in enumerate((x, y, z, x * x + y * y + z * z)):
            first = value.astype(BF).astype(F)
            rest = value - first
            second = rest.astype(BF).astype(F)
            third = rest - second
            for k, part in enumerate((first, second, third, first, second, first)):
                v_ref[buf, pl.ds((f * 6 + k) * 8, 8), :] = part
        for j in range(SLOTS):
            v = [v_ref[buf, pl.ds(n * 64 + j, 8, stride=8), :] for n in range(4)]
            b_ref[buf, j] = jnp.concatenate(v, 0).astype(BF)

    def stage1(i, buf, j):
        i = jnp.minimum(i, DEVICES - 1)
        g = ((surf - i) & 3) * BOX_DEV + ids_ref[j, i]
        a = a_ref[pl.ds(pl.multiple_of(g * FEATS, FEATS), FEATS), :]
        q_ref[buf, j] = lax.dot_general(
            a, b_ref[buf, j], (((0,), (0,)), ((), ())), preferred_element_type=F
        )

    def stage2(buf, j):
        m = jnp.maximum(q_ref[buf, j], TINY)
        q = m * lax.rsqrt(m)
        t = jnp.maximum(1.0 - q, 0.0)
        t = t * t
        w = (t * t) * (q + 0.25)
        high = w.astype(BF)
        w_ref[buf, j, 0:128, :] = high
        w_ref[buf, j, 128:256, :] = (w - high.astype(F)).astype(BF)

    def stage3(i, buf, j):
        g = ((surf - i) & 3) * BOX_DEV + ids_ref[j, i]
        c = cf_ref[pl.ds(pl.multiple_of(g * 16, 16), 16), :]
        c = jnp.concatenate([c, c], 1)
        r = jnp.dot(c, w_ref[buf, j], preferred_element_type=F)
        r_ref[buf, pl.ds(j, 6, stride=SLOTS), :] = r[0:6]

    def stage4(i, buf):
        base = pl.multiple_of(i * GIVE, GIVE)
        o_ref[pl.ds(base, GIVE), :] = r_ref[buf, 0:GIVE, :] + r_ref[buf, GIVE : 2 * GIVE, :]

    slots = range(SLOTS)
    stage0(0, 0)
    stage0(1, 1)
    a_copy.wait()
    for j in slots:
        stage1(0, 0, j)
    stage0(2, 0)
    for j in slots:
        stage1(1, 1, j)
    for j in slots:
        stage2(0, j)
    c_copy.wait()

    def some(h, carry):
        for u in range(UNROLL):
            i = h * UNROLL + u
            buf = u % 2
            for j in slots:
                stage1(i + 2, buf, j)
                stage2(1 - buf, j)
                stage3(i, buf, j)
            stage4(i, buf)
            stage0(i + 3, 1 - buf)
        return carry

    lax.fori_loop(0, DEVICES // UNROLL, some, 0)


def sum_kernel(list_ref, back_ref, o_ref):
    _, slot = slot_table(list_ref[...])
    acc = jnp.zeros((BOX_DEV, 384), F)
    for j in range(SLOTS):
        sel = (slot == float(j)).astype(F).astype(BF)
        terms = jnp.concatenate(
            [back_ref[pl.ds(c * SLOTS + j, DEVICES, stride=GIVE), :] for c in range(3)], 1
        )
        for part in split3(terms):
            acc = acc + jnp.dot(sel, part.astype(BF), preferred_element_type=F)
    for c in range(3):
        o_ref[c * BOX_DEV : (c + 1) * BOX_DEV, :] = acc[:, c * 128 : (c + 1) * 128]


def reduce_kernel(node_ref, own_ref, one_ref, two_ref, three_ref, d_ref, up_ref, down_ref):
    d_ref[...] = own_ref[...] + one_ref[...] + two_ref[...] + three_ref[...]
    zero = jnp.zeros((HALO, 128), F)
    x = [node_ref[c] for c in range(3)]
    d = [d_ref[c * BOX_DEV : (c + 1) * BOX_DEV, :] for c in range(3)]
    for ref, first in ((up_ref, BOX_DEV - HALO), (down_ref, 0)):
        ref[...] = jnp.concatenate([t[first : first + HALO] for t in x + d] + [zero, zero], 0)


def corners(near_ref, tab_ref, code_ref, cor_ref, box, at, origin, count):
    tables = []
    for j in range(8):
        row = near_ref[j, box] - origin
        tables.append(tab_ref[pl.ds(pl.multiple_of(row * 8, 8), 8), :])
    for h in range(2):
        for k in range(3):
            code = code_ref[pl.ds((k * 2 + h) * BOX_DEV + box, 1), :]
            code = jnp.broadcast_to(code, (8, 128))
            lane = code & 127
            which = code >> 7
            got = None
            for j in range(8):
                value = jnp.take_along_axis(tables[j], lane, axis=1)
                got = value if got is None else jnp.where(which == j, value, got)
            cor_ref[k, pl.ds(h * count + at, 8, stride=2 * count), :] = got


def volumes(refs, h, count):
    def corner(k):
        part = [ref[k, pl.ds((c * 2 + h) * count, count), :] for ref in refs for c in range(6 // len(refs))]
        return [part[c] + 0.5 * part[c + 3] for c in range(3)], part[3:6]

    (ma, da), (mb, db), (mc, dc) = corner(0), corner(1), corner(2)
    u = [mb[c] - ma[c] for c in range(3)]
    w = [mc[c] - ma[c] for c in range(3)]
    swept = None
    for c in range(3):
        p, q = (c + 1) % 3, (c + 2) % 3
        normal = 0.5 * (u[p] * w[q] - u[q] * w[p])
        term = ((da[c] + db[c] + dc[c]) / 3.0) * normal
        swept = term if swept is None else swept + term
    return swept


def split_codes(face_ref, code_ref):
    for k in range(3):
        for h in range(2):
            code_ref[pl.ds((k * 2 + h) * BOX_DEV, BOX_DEV), :] = face_ref[
                k, :, h * 128 : (h + 1) * 128
            ]


def gather_three(near_ref, face_ref, rows, origin, put, tab_ref, code_ref):
    zero = jnp.zeros((BOX_DEV, 128), F)
    for half in range(2):
        for c in range(4):
            tab_ref[pl.ds(half * 4 + c, BOX_DEV, stride=8), :] = rows[c] if c < 3 else zero
    split_codes(face_ref, code_ref)
    upper = lax.broadcasted_iota(I, (8, 128), 0) >= 4

    def some(g, carry):
        for u in range(8):
            box = g * 8 + HALO + u
            tables = []
            for j in range(8):
                row = near_ref[j, box] - origin
                tables.append(tab_ref[pl.ds(pl.multiple_of(row * 8, 8), 8), :])
            tables = [jnp.where(upper, tables[j + 4], tables[j]) for j in range(4)]
            for h in range(2):
                for k in range(3):
                    code = code_ref[pl.ds((k * 2 + h) * BOX_DEV + box, 1), :]
                    code = jnp.broadcast_to(code, (8, 128))
                    lane = code & 127
                    which = (code >> 7) & 3
                    got = None
                    for j in range(4):
                        value = jnp.take_along_axis(tables[j], lane, axis=1)
                        got = value if got is None else jnp.where(which == j, value, got)
                    got = jnp.where(code >= 512, pltpu.roll(got, 4, 0), got)
                    put[k, pl.ds(h * BOX_DEV + box, 3, stride=2 * BOX_DEV), :] = got[0:3]
        return carry

    lax.fori_loop(0, (BOX_DEV - 2 * HALO) // 8, some, 0)


def place_kernel(where_ref, near_ref, node_ref, face_ref, o_ref, tab_ref, code_ref):
    rows = [node_ref[c] for c in range(3)]
    gather_three(near_ref, face_ref, rows, where_ref[0] * BOX_DEV, o_ref, tab_ref, code_ref)


def inner_kernel(where_ref, near_ref, d_ref, place_ref, face_ref, v_ref, s_ref, tab_ref, cor_ref, code_ref):
    rows = [d_ref[c * BOX_DEV : (c + 1) * BOX_DEV, :] for c in range(3)]
    gather_three(near_ref, face_ref, rows, where_ref[0] * BOX_DEV, cor_ref, tab_ref, code_ref)
    for h in range(2):
        s_ref[:, h * 128 : (h + 1) * 128] = volumes((place_ref, cor_ref), h, BOX_DEV)
    for c in range(3):
        v_ref[c] = d_ref[c * BOX_DEV : (c + 1) * BOX_DEV, :] * 2.0


def edge_kernel(
    where_ref, near_ref, node_ref, d_ref, low_ref, high_ref, face_ref, in_ref, s_ref, tab_ref, cor_ref, code_ref
):
    for c in range(6):
        own = node_ref[c] if c < 3 else d_ref[(c - 3) * BOX_DEV : (c - 2) * BOX_DEV, :]
        edge = slice(c * HALO, (c + 1) * HALO)
        tab_ref[pl.ds(c, NEAR, stride=8), :] = jnp.concatenate(
            [low_ref[edge, :], own, high_ref[edge, :]], 0
        )
    for c in (6, 7):
        tab_ref[pl.ds(c, NEAR, stride=8), :] = jnp.zeros((NEAR, 128), F)
    split_codes(face_ref, code_ref)
    origin = where_ref[0] * BOX_DEV - HALO
    for at in range(2 * HALO):
        box = at if at < HALO else BOX_DEV - 2 * HALO + at
        corners(near_ref, tab_ref, code_ref, cor_ref, box, at, origin, 2 * HALO)
    s_ref[...] = in_ref[...]
    for h in range(2):
        swept = volumes((cor_ref,), h, 2 * HALO)
        s_ref[0:HALO, h * 128 : (h + 1) * 128] = swept[0:HALO]
        s_ref[BOX_DEV - HALO : BOX_DEV, h * 128 : (h + 1) * 128] = swept[HALO:]


def to_all(array):
    peers = DEVICES // 4
    rows = array.shape[0] // peers
    packets = array.reshape(peers, rows, 1, 128)
    packets = lax.all_to_all(packets, "vol", split_axis=0, concat_axis=0, tiled=True)
    return packets.reshape(peers * rows, 128)


def around(array):
    return [lax.ppermute(array, "surf", [(i, (i + k) % 4) for i in range(4)]) for k in (1, 2, 3)]


def shape(*dims, kind=F):
    return jax.ShapeDtypeStruct(dims, kind)


def body(node_pos, centres, coefs, radii, block_list, neighbours, faces):
    listed = block_list[0].T
    nodes, cens, weights = [a.transpose(1, 0, 2) for a in (node_pos, centres, coefs)]
    where = jnp.stack([lax.axis_index("vol"), lax.axis_index("surf")]).astype(I)
    blocks = jnp.concatenate(
        [cens.reshape(3 * BOX_DEV, 128), radii, weights.reshape(3 * BOX_DEV, 128)], 0
    )
    (sent,) = call(
        prep_kernel,
        "prep",
        (pltpu.HBM((DEVICES * ASK, 128), F),),
        [("f", pltpu.with_memory_space_constraint(a, pltpu.HBM)) for a in (listed, nodes)],
        [
            pltpu.VMEM(listed.shape, I),
            pltpu.VMEM(nodes.shape, F),
            pltpu.VMEM((DEVICES // 2 * ASK, 128), F),
            pltpu.VMEM((DEVICES // 2 * ASK, 128), F),
            pltpu.SemaphoreType.DMA((4,)),
        ],
        out=FAR,
    )
    near, codes = neighbours.T, faces.transpose(1, 0, 2)
    sent, early = lax.optimization_barrier((sent, codes))
    (place,) = call(
        place_kernel,
        "place",
        (shape(3, 6 * BOX_DEV, 128),),
        [("s", where), ("s", near), ("v", nodes), ("v", early)],
        [pltpu.VMEM((8 * BOX_DEV, 128), F), pltpu.VMEM((6 * BOX_DEV, 128), I)],
        us=4,
    )
    sizes = (4 * BOX_DEV * FEATS, 128), (4 * BOX_DEV * 16, 128)
    tables = call(
        feat_kernel,
        "feats",
        tuple(pltpu.HBM(size, BF) for size in sizes),
        [("v", blocks)] + [("v", r) for r in around(blocks)],
        [pltpu.VMEM(size, BF) for size in sizes] + [pltpu.SemaphoreType.DMA((8,))],
        us=5,
        out=FAR,
    )
    (terms,) = call(
        terms_kernel,
        "terms",
        (shape(DEVICES * GIVE, 128),),
        [("s", where), ("v", to_all(sent))] + [("f", pltpu.with_memory_space_constraint(t, pltpu.HBM)) for t in tables],
        [
            pltpu.VMEM((4 * BOX_DEV * FEATS, 128), BF),
            pltpu.VMEM((4 * BOX_DEV * 16, 128), BF),
            pltpu.VMEM((2, 8 * FEATS, 128), F),
            pltpu.VMEM((2, SLOTS, FEATS, 128), BF),
            pltpu.VMEM((2, SLOTS, 128, 128), F),
            pltpu.VMEM((2, SLOTS, 256, 128), BF),
            pltpu.VMEM((2, 2 * GIVE, 128), F),
            pltpu.VMEM((SLOTS, 128), I),
            pltpu.SMEM((SLOTS, 128), I),
            pltpu.SemaphoreType.DMA,
            pltpu.SemaphoreType.DMA,
            pltpu.SemaphoreType.DMA,
        ],
        mib=16,
        us=45,
    )
    (own,) = call(
        sum_kernel,
        "sums",
        (shape(3 * BOX_DEV, 128),),
        [("v", listed), ("v", to_all(terms))],
    )
    d, up, down = call(
        reduce_kernel,
        "reduce",
        (shape(3 * BOX_DEV, 128), shape(32, 128), shape(32, 128)),
        [("v", nodes), ("v", own)] + [("v", r) for r in around(own)],
    )
    low = lax.ppermute(up, "vol", [(i, i + 1) for i in range(31)])
    high = lax.ppermute(down, "vol", [(i + 1, i) for i in range(31)])
    velocity, inner = call(
        inner_kernel,
        "inner",
        (shape(3, BOX_DEV, 128), shape(BOX_DEV, 256)),
        [("s", where), ("s", near), ("v", d), ("v", place), ("v", codes)],
        [
            pltpu.VMEM((8 * BOX_DEV, 128), F),
            pltpu.VMEM((3, 6 * BOX_DEV, 128), F),
            pltpu.VMEM((6 * BOX_DEV, 128), I),
        ],
        us=4,
    )
    (swept,) = call(
        edge_kernel,
        "edges",
        (shape(BOX_DEV, 256),),
        [("s", where), ("s", near), ("v", nodes), ("v", d), ("v", low), ("v", high), ("v", codes), ("v", inner)],
        [
            pltpu.VMEM((8 * NEAR, 128), F),
            pltpu.VMEM((3, 128, 128), F),
            pltpu.VMEM((6 * BOX_DEV, 128), I),
        ],
    )
    return velocity.transpose(1, 0, 2), swept


def solution(mesh):
    placed = (
        P("vol", None, None),
        P(("vol", "surf"), None, None),
        P(("vol", "surf"), None, None),
        P(("vol", "surf"), None),
        P("surf", "vol", None),
        P("vol", None),
        P("vol", None, None),
    )
    return jax.shard_map(
        body,
        mesh=mesh,
        in_specs=placed,
        out_specs=(P("vol", None, None), P("vol", None)),
        check_vma=False,
    )
```

```python
import functools

import jax
import jax.numpy as jnp
from jax import lax
from jax.experimental import pallas as pl
from jax.experimental.pallas import tpu as pltpu
from jax.sharding import PartitionSpec as P

BF = jnp.bfloat16
F = jnp.float32
I = jnp.int32
BOTH = ("vol", "surf")
DEVICES = 128
SLOTS = 8
ASK = 3 * SLOTS + 1
GIVE = 3 * SLOTS
FEATS = 32
UNROLL = 8
BOX_DEV = 64
HALO = 4
NEAR = BOX_DEV + 2 * HALO
TINY = 1e-30
VMEM = pl.BlockSpec(memory_space=pltpu.VMEM)
SMEM = pl.BlockSpec(memory_space=pltpu.SMEM)
FAR = pl.BlockSpec(memory_space=pltpu.HBM)
SPACES = {"v": VMEM, "s": SMEM, "f": FAR}


def call(kernel, name, outs, ins, scratch=(), mib=8, us=2, out=VMEM):
    specs = [SPACES[space] for space, _ in ins]
    return pl.pallas_call(
        kernel,
        name=name,
        out_shape=outs,
        in_specs=specs,
        out_specs=tuple(out for _ in outs),
        scratch_shapes=list(scratch),
        compiler_params=pltpu.CompilerParams(vmem_limit_bytes=mib << 20),
        cost_estimate=pl.CostEstimate(flops=us * 10**9, bytes_accessed=us * 10**6, transcendentals=0),
    )(*[array for _, array in ins])


def split3(x):
    first = x.astype(BF).astype(F)
    rest = x - first
    second = rest.astype(BF).astype(F)
    return first, second, (rest - second).astype(BF).astype(F)


def slot_table(listed):
    listed = listed.astype(F).T.astype(I)
    owner = listed >> 6
    local = (listed & 63) + 1
    lanes = lax.broadcasted_iota(I, (BOX_DEV, DEVICES), 1)
    table = jnp.zeros((BOX_DEV, DEVICES), I)
    for k in range(listed.shape[1]):
        hit = owner[:, k : k + 1] == lanes
        table = jnp.where(hit, local[:, k : k + 1], table)
    table = table.astype(F)
    used = table > 0.0
    row = lax.broadcasted_iota(I, (BOX_DEV, BOX_DEV), 0)
    col = lax.broadcasted_iota(I, (BOX_DEV, BOX_DEV), 1)
    before = (col < row).astype(F).astype(BF)
    rank = jnp.dot(before, used.astype(F).astype(BF), preferred_element_type=F)
    return table, jnp.where(used, rank, -1.0)


def prep_kernel(list_far, node_far, o_far, list_ref, node_ref, low_ref, high_ref, sems):
    list_copy = pltpu.make_async_copy(list_far, list_ref, sems.at[0])
    node_copy = pltpu.make_async_copy(node_far, node_ref, sems.at[1])
    list_copy.start()
    node_copy.start()
    list_copy.wait()
    table, slot = slot_table(list_ref[...])
    slot_t = slot.T
    ids = [
        jnp.sum(jnp.where(slot == float(j), table - 1.0, 0.0), axis=0, keepdims=True)
        for j in range(SLOTS)
    ]
    stacked = jnp.concatenate(ids + [jnp.zeros((128 - SLOTS, 128), F)], 0).T
    node_copy.wait()
    nodes = jnp.concatenate([node_ref[c] for c in range(3)], 1)
    parts = [p.astype(BF) for p in split3(nodes)]
    owners = DEVICES // 2
    copies = []
    for half, ref in enumerate((low_ref, high_ref)):
        rows = slice(half * owners, (half + 1) * owners)
        for j in range(SLOTS):
            sel = (slot_t[rows] == float(j)).astype(F).astype(BF)
            got = sum(jnp.dot(sel, p, preferred_element_type=F) for p in parts)
            for c in range(3):
                ref[pl.ds(c * SLOTS + j, owners, stride=ASK), :] = got[:, c * 128 : (c + 1) * 128]
        ref[pl.ds(ASK - 1, owners, stride=ASK), :] = stacked[rows]
        part = pl.ds(half * owners * ASK, owners * ASK)
        copies.append(pltpu.make_async_copy(ref, o_far.at[part, :], sems.at[2 + half]))
        copies[half].start()
    for copy in copies:
        copy.wait()


def feat_kernel(own_ref, one_ref, two_ref, three_ref, far_ref, farc_ref, a_ref, cf_ref, sems):
    copies = []
    for k, ref in enumerate((own_ref, one_ref, two_ref, three_ref)):
        first = k * BOX_DEV

        def some(h, carry):
            base = pl.multiple_of(h * 8, 8)
            x, y, z, r, kx, ky, kz = [ref[pl.ds(c * BOX_DEV + base, 8), :] for c in range(7)]
            inv = 1.0 / (r * r)
            scale = -2.0 * inv
            rows = [x * scale, y * scale, z * scale, inv, inv * (x * x + y * y + z * z)]
            rows = [split3(t) for t in rows]
            ks = [split3(4.0 * t) for t in (kx, ky, kz)]
            for u in range(8):
                s = [t[n][u : u + 1] for t in rows[0:4] for n in (0, 0, 0, 1, 1, 2)]
                s += [rows[4][n][u : u + 1] for n in range(3)] + [jnp.zeros((5, 128), F)]
                at = first + base + u
                a_ref[pl.ds(pl.multiple_of(at * FEATS, FEATS), FEATS), :] = jnp.concatenate(s, 0).astype(BF)
                c = jnp.concatenate(
                    [t[n][u : u + 1] for n in range(2) for t in ks] + [jnp.zeros((10, 128), F)], 0
                ).astype(BF)
                cf_ref[pl.ds(pl.multiple_of(at * 16, 16), 16), :] = c
            return carry

        lax.fori_loop(0, BOX_DEV // 8, some, 0)
        for n, (near, far, height) in enumerate(((a_ref, far_ref, FEATS), (cf_ref, farc_ref, 16))):
            part = pl.ds(first * height, BOX_DEV * height)
            copy = pltpu.make_async_copy(near.at[part, :], far.at[part, :], sems.at[2 * k + n])
            copy.start()
            copies.append(copy)
    for copy in copies:
        copy.wait()


def terms_kernel(
    where_ref, x_ref, far_ref, farc_ref, o_ref, a_ref, cf_ref, v_ref, b_ref, q_ref, w_ref, r_ref, stage_ref, ids_ref, sem, a_sem, c_sem
):
    a_copy = pltpu.make_async_copy(far_ref, a_ref, a_sem)
    c_copy = pltpu.make_async_copy(farc_ref, cf_ref, c_sem)
    a_copy.start()
    c_copy.start()
    stage_ref[...] = x_ref[pl.ds(ASK - 1, DEVICES, stride=ASK), :].T[0:SLOTS].astype(I)
    copy = pltpu.make_async_copy(stage_ref, ids_ref, sem)
    copy.start()
    for buf in range(2):
        v_ref[buf, pl.ds(192, 24), :] = jnp.ones((24, 128), F)
        v_ref[buf, pl.ds(216, 40), :] = jnp.zeros((40, 128), F)
    copy.wait()
    surf = where_ref[1]

    def stage0(i, buf):
        i = jnp.minimum(i, DEVICES - 1)
        base = i * ASK
        x, y, z = [x_ref[pl.ds(base + c * SLOTS, SLOTS), :] for c in range(3)]
        for f, value in enumerate((x, y, z, x * x + y * y + z * z)):
            first = value.astype(BF).astype(F)
            rest = value - first
            second = rest.astype(BF).astype(F)
            third = rest - second
            for k, part in enumerate((first, second, third, first, second, first)):
                v_ref[buf, pl.ds((f * 6 + k) * 8, 8), :] = part
        for j in range(SLOTS):
            v = [v_ref[buf, pl.ds(n * 64 + j, 8, stride=8), :] for n in range(4)]
            b_ref[buf, j] = jnp.concatenate(v, 0).astype(BF)

    def stage1(i, buf, j):
        i = jnp.minimum(i, DEVICES - 1)
        g = ((surf - i) & 3) * BOX_DEV + ids_ref[j, i]
        a = a_ref[pl.ds(pl.multiple_of(g * FEATS, FEATS), FEATS), :]
        q_ref[buf, j] = lax.dot_general(
            a, b_ref[buf, j], (((0,), (0,)), ((), ())), preferred_element_type=F
        )

    def stage2(buf, j):
        m = jnp.maximum(q_ref[buf, j], TINY)
        q = m * lax.rsqrt(m)
        t = jnp.maximum(1.0 - q, 0.0)
        t = t * t
        w = (t * t) * (q + 0.25)
        high = w.astype(BF)
        w_ref[buf, j, 0:128, :] = high
        w_ref[buf, j, 128:256, :] = (w - high.astype(F)).astype(BF)

    def stage3(i, buf, j):
        g = ((surf - i) & 3) * BOX_DEV + ids_ref[j, i]
        c = cf_ref[pl.ds(pl.multiple_of(g * 16, 16), 16), :]
        c = jnp.concatenate([c, c], 1)
        r = jnp.dot(c, w_ref[buf, j], preferred_element_type=F)
        r_ref[buf, pl.ds(j, 6, stride=SLOTS), :] = r[0:6]

    def stage4(i, buf):
        base = pl.multiple_of(i * GIVE, GIVE)
        o_ref[pl.ds(base, GIVE), :] = r_ref[buf, 0:GIVE, :] + r_ref[buf, GIVE : 2 * GIVE, :]

    slots = range(SLOTS)
    stage0(0, 0)
    stage0(1, 1)
    a_copy.wait()
    for j in slots:
        stage1(0, 0, j)
    stage0(2, 0)
    for j in slots:
        stage1(1, 1, j)
    for j in slots:
        stage2(0, j)
    c_copy.wait()

    def some(h, carry):
        for u in range(UNROLL):
            i = h * UNROLL + u
            buf = u % 2
            for j in slots:
                stage1(i + 2, buf, j)
                stage2(1 - buf, j)
                stage3(i, buf, j)
            stage4(i, buf)
            stage0(i + 3, 1 - buf)
        return carry

    lax.fori_loop(0, DEVICES // UNROLL, some, 0)


def sum_kernel(list_ref, back_ref, o_ref):
    _, slot = slot_table(list_ref[...])
    acc = jnp.zeros((BOX_DEV, 384), F)
    for j in range(SLOTS):
        sel = (slot == float(j)).astype(F).astype(BF)
        terms = jnp.concatenate(
            [back_ref[pl.ds(c * SLOTS + j, DEVICES, stride=GIVE), :] for c in range(3)], 1
        )
        for part in split3(terms)[0:2]:
            acc = acc + jnp.dot(sel, part.astype(BF), preferred_element_type=F)
    for c in range(3):
        o_ref[c * BOX_DEV : (c + 1) * BOX_DEV, :] = acc[:, c * 128 : (c + 1) * 128]


def reduce_kernel(node_ref, own_ref, one_ref, two_ref, three_ref, d_ref, up_ref, down_ref):
    d_ref[...] = own_ref[...] + one_ref[...] + two_ref[...] + three_ref[...]
    zero = jnp.zeros((HALO, 128), F)
    x = [node_ref[c] for c in range(3)]
    d = [d_ref[c * BOX_DEV : (c + 1) * BOX_DEV, :] for c in range(3)]
    for ref, first in ((up_ref, BOX_DEV - HALO), (down_ref, 0)):
        ref[...] = jnp.concatenate([t[first : first + HALO] for t in x + d] + [zero, zero], 0)


def corners(near_ref, tab_ref, code_ref, cor_ref, box, at, origin, count):
    tables = []
    for j in range(8):
        row = near_ref[j, box] - origin
        tables.append(tab_ref[pl.ds(pl.multiple_of(row * 8, 8), 8), :])
    for h in range(2):
        for k in range(3):
            code = code_ref[pl.ds((k * 2 + h) * BOX_DEV + box, 1), :]
            code = jnp.broadcast_to(code, (8, 128))
            lane = code & 127
            which = code >> 7
            got = None
            for j in range(8):
                value = jnp.take_along_axis(tables[j], lane, axis=1)
                got = value if got is None else jnp.where(which == j, value, got)
            cor_ref[k, pl.ds(h * count + at, 8, stride=2 * count), :] = got


def volumes(refs, h, count):
    def corner(k):
        part = [ref[k, pl.ds((c * 2 + h) * count, count), :] for ref in refs for c in range(6 // len(refs))]
        return [part[c] + 0.5 * part[c + 3] for c in range(3)], part[3:6]

    (ma, da), (mb, db), (mc, dc) = corner(0), corner(1), corner(2)
    u = [mb[c] - ma[c] for c in range(3)]
    w = [mc[c] - ma[c] for c in range(3)]
    swept = None
    for c in range(3):
        p, q = (c + 1) % 3, (c + 2) % 3
        normal = 0.5 * (u[p] * w[q] - u[q] * w[p])
        term = ((da[c] + db[c] + dc[c]) / 3.0) * normal
        swept = term if swept is None else swept + term
    return swept


def split_codes(face_ref, code_ref):
    for k in range(3):
        for h in range(2):
            code_ref[pl.ds((k * 2 + h) * BOX_DEV, BOX_DEV), :] = face_ref[
                k, :, h * 128 : (h + 1) * 128
            ]


def gather_three(near_ref, face_ref, rows, origin, put, tab_ref, code_ref):
    zero = jnp.zeros((BOX_DEV, 128), F)
    for half in range(2):
        for c in range(4):
            tab_ref[pl.ds(half * 4 + c, BOX_DEV, stride=8), :] = rows[c] if c < 3 else zero
    split_codes(face_ref, code_ref)
    upper = lax.broadcasted_iota(I, (8, 128), 0) >= 4

    def some(g, carry):
        for u in range(8):
            box = g * 8 + HALO + u
            tables = []
            for j in range(8):
                row = near_ref[j, box] - origin
                tables.append(tab_ref[pl.ds(pl.multiple_of(row * 8, 8), 8), :])
            tables = [jnp.where(upper, tables[j + 4], tables[j]) for j in range(4)]
            for h in range(2):
                for k in range(3):
                    code = code_ref[pl.ds((k * 2 + h) * BOX_DEV + box, 1), :]
                    code = jnp.broadcast_to(code, (8, 128))
                    lane = code & 127
                    which = (code >> 7) & 3
                    got = None
                    for j in range(4):
                        value = jnp.take_along_axis(tables[j], lane, axis=1)
                        got = value if got is None else jnp.where(which == j, value, got)
                    got = jnp.where(code >= 512, pltpu.roll(got, 4, 0), got)
                    put[k, pl.ds(h * BOX_DEV + box, 3, stride=2 * BOX_DEV), :] = got[0:3]
        return carry

    lax.fori_loop(0, (BOX_DEV - 2 * HALO) // 8, some, 0)


def place_kernel(where_ref, near_ref, node_ref, face_ref, o_ref, tab_ref, code_ref):
    rows = [node_ref[c] for c in range(3)]
    gather_three(near_ref, face_ref, rows, where_ref[0] * BOX_DEV, o_ref, tab_ref, code_ref)


def inner_kernel(where_ref, near_ref, d_ref, place_ref, face_ref, v_ref, s_ref, tab_ref, cor_ref, code_ref):
    rows = [d_ref[c * BOX_DEV : (c + 1) * BOX_DEV, :] for c in range(3)]
    gather_three(near_ref, face_ref, rows, where_ref[0] * BOX_DEV, cor_ref, tab_ref, code_ref)
    for h in range(2):
        s_ref[:, h * 128 : (h + 1) * 128] = volumes((place_ref, cor_ref), h, BOX_DEV)
    for c in range(3):
        v_ref[c] = d_ref[c * BOX_DEV : (c + 1) * BOX_DEV, :] * 2.0


def edge_kernel(
    where_ref, near_ref, node_ref, d_ref, low_ref, high_ref, face_ref, in_ref, s_ref, tab_ref, cor_ref, code_ref
):
    for c in range(6):
        own = node_ref[c] if c < 3 else d_ref[(c - 3) * BOX_DEV : (c - 2) * BOX_DEV, :]
        edge = slice(c * HALO, (c + 1) * HALO)
        tab_ref[pl.ds(c, NEAR, stride=8), :] = jnp.concatenate(
            [low_ref[edge, :], own, high_ref[edge, :]], 0
        )
    for c in (6, 7):
        tab_ref[pl.ds(c, NEAR, stride=8), :] = jnp.zeros((NEAR, 128), F)
    split_codes(face_ref, code_ref)
    origin = where_ref[0] * BOX_DEV - HALO
    for at in range(2 * HALO):
        box = at if at < HALO else BOX_DEV - 2 * HALO + at
        corners(near_ref, tab_ref, code_ref, cor_ref, box, at, origin, 2 * HALO)
    s_ref[...] = in_ref[...]
    for h in range(2):
        swept = volumes((cor_ref,), h, 2 * HALO)
        s_ref[0:HALO, h * 128 : (h + 1) * 128] = swept[0:HALO]
        s_ref[BOX_DEV - HALO : BOX_DEV, h * 128 : (h + 1) * 128] = swept[HALO:]


def to_all(array):
    peers = DEVICES // 4
    rows = array.shape[0] // peers
    packets = array.reshape(peers, rows, 1, 128)
    packets = lax.all_to_all(packets, "vol", split_axis=0, concat_axis=0, tiled=True)
    return packets.reshape(peers * rows, 128)


def around(array):
    return [lax.ppermute(array, "surf", [(i, (i + k) % 4) for i in range(4)]) for k in (1, 2, 3)]


def shape(*dims, kind=F):
    return jax.ShapeDtypeStruct(dims, kind)


def body(node_pos, centres, coefs, radii, block_list, neighbours, faces):
    listed = block_list[0].T
    nodes, cens, weights = [a.transpose(1, 0, 2) for a in (node_pos, centres, coefs)]
    where = jnp.stack([lax.axis_index("vol"), lax.axis_index("surf")]).astype(I)
    blocks = jnp.concatenate(
        [cens.reshape(3 * BOX_DEV, 128), radii, weights.reshape(3 * BOX_DEV, 128)], 0
    )
    (sent,) = call(
        prep_kernel,
        "prep",
        (pltpu.HBM((DEVICES * ASK, 128), F),),
        [("f", pltpu.with_memory_space_constraint(a, pltpu.HBM)) for a in (listed, nodes)],
        [
            pltpu.VMEM(listed.shape, I),
            pltpu.VMEM(nodes.shape, F),
            pltpu.VMEM((DEVICES // 2 * ASK, 128), F),
            pltpu.VMEM((DEVICES // 2 * ASK, 128), F),
            pltpu.SemaphoreType.DMA((4,)),
        ],
        out=FAR,
    )
    near, codes = neighbours.T, faces.transpose(1, 0, 2)
    sent, early = lax.optimization_barrier((sent, codes))
    (place,) = call(
        place_kernel,
        "place",
        (shape(3, 6 * BOX_DEV, 128),),
        [("s", where), ("s", near), ("v", nodes), ("v", early)],
        [pltpu.VMEM((8 * BOX_DEV, 128), F), pltpu.VMEM((6 * BOX_DEV, 128), I)],
        us=4,
    )
    sizes = (4 * BOX_DEV * FEATS, 128), (4 * BOX_DEV * 16, 128)
    tables = call(
        feat_kernel,
        "feats",
        tuple(pltpu.HBM(size, BF) for size in sizes),
        [("v", blocks)] + [("v", r) for r in around(blocks)],
        [pltpu.VMEM(size, BF) for size in sizes] + [pltpu.SemaphoreType.DMA((8,))],
        us=5,
        out=FAR,
    )
    (terms,) = call(
        terms_kernel,
        "terms",
        (shape(DEVICES * GIVE, 128),),
        [("s", where), ("v", to_all(sent))] + [("f", pltpu.with_memory_space_constraint(t, pltpu.HBM)) for t in tables],
        [
            pltpu.VMEM((4 * BOX_DEV * FEATS, 128), BF),
            pltpu.VMEM((4 * BOX_DEV * 16, 128), BF),
            pltpu.VMEM((2, 8 * FEATS, 128), F),
            pltpu.VMEM((2, SLOTS, FEATS, 128), BF),
            pltpu.VMEM((2, SLOTS, 128, 128), F),
            pltpu.VMEM((2, SLOTS, 256, 128), BF),
            pltpu.VMEM((2, 2 * GIVE, 128), F),
            pltpu.VMEM((SLOTS, 128), I),
            pltpu.SMEM((SLOTS, 128), I),
            pltpu.SemaphoreType.DMA,
            pltpu.SemaphoreType.DMA,
            pltpu.SemaphoreType.DMA,
        ],
        mib=16,
        us=45,
    )
    (own,) = call(
        sum_kernel,
        "sums",
        (shape(3 * BOX_DEV, 128),),
        [("v", listed), ("v", to_all(terms))],
    )
    d, up, down = call(
        reduce_kernel,
        "reduce",
        (shape(3 * BOX_DEV, 128), shape(32, 128), shape(32, 128)),
        [("v", nodes), ("v", own)] + [("v", r) for r in around(own)],
    )
    low = lax.ppermute(up, "vol", [(i, i + 1) for i in range(31)])
    high = lax.ppermute(down, "vol", [(i + 1, i) for i in range(31)])
    velocity, inner = call(
        inner_kernel,
        "inner",
        (shape(3, BOX_DEV, 128), shape(BOX_DEV, 256)),
        [("s", where), ("s", near), ("v", d), ("v", place), ("v", codes)],
        [
            pltpu.VMEM((8 * BOX_DEV, 128), F),
            pltpu.VMEM((3, 6 * BOX_DEV, 128), F),
            pltpu.VMEM((6 * BOX_DEV, 128), I),
        ],
        us=4,
    )
    (swept,) = call(
        edge_kernel,
        "edges",
        (shape(BOX_DEV, 256),),
        [("s", where), ("s", near), ("v", nodes), ("v", d), ("v", low), ("v", high), ("v", codes), ("v", inner)],
        [
            pltpu.VMEM((8 * NEAR, 128), F),
            pltpu.VMEM((3, 128, 128), F),
            pltpu.VMEM((6 * BOX_DEV, 128), I),
        ],
    )
    return velocity.transpose(1, 0, 2), swept


def solution(mesh):
    placed = (
        P("vol", None, None),
        P(("vol", "surf"), None, None),
        P(("vol", "surf"), None, None),
        P(("vol", "surf"), None),
        P("surf", "vol", None),
        P("vol", None),
        P("vol", None, None),
    )
    return jax.shard_map(
        body,
        mesh=mesh,
        in_specs=placed,
        out_specs=(P("vol", None, None), P("vol", None)),
        check_vma=False,
    )
```
